32 devices in a mesh: dp: 16 (over z, y, core), tensor: 2 (over x).
Axes of the slice: x: 2, y: 2, z: 4, core: 2. Of those that a mesh axis runs over, the one named last changes fastest.
Arguments:
- tokens: bfloat16 [32768, 1024], P(('dp', 'tensor')), may hold values from -40 to 40
- gain_mix: float32 [1024], replicated, may hold values from 0.1 to 1.9
- in_weight: bfloat16 [3, 1024, 1024], P(None, 'dp', 'tensor'), may hold values from -0.1875 to 0.1875
- conv_weight: float32 [3, 1024], replicated, may hold values from -3 to 3
- out_weight: bfloat16 [1024, 1024], P('dp', 'tensor'), may hold values from -0.1875 to 0.1875
- gain_ff: float32 [1024], replicated, may hold values from 0.1 to 1.9
- gate_up_weight: bfloat16 [2, 1024, 4608], P(None, 'dp', 'tensor'), may hold values from -0.1875 to 0.1875
- down_weight: bfloat16 [1024, 4608], P('dp', 'tensor'), may hold values from -0.09375 to 0.09375
- grad_out: bfloat16 [32768, 1024], P(('dp', 'tensor')), may hold values from -9 to 9
Outputs:
- block_out: bfloat16 [32768, 1024], P(('dp', 'tensor'))
- input_grad: float32 [32768, 1024], P(('dp', 'tensor'))
- gain_mix_grad: float32 [1024], replicated
- in_weight_grad: float32 [3, 1024, 1024], P(None, 'dp', 'tensor')
- conv_weight_grad: float32 [3, 1024], replicated
- out_weight_grad: float32 [1024, 1024], P('dp', 'tensor')
- gain_ff_grad: float32 [1024], replicated
- gate_up_weight_grad: float32 [2, 1024, 4608], P(None, 'dp', 'tensor')
- down_weight_grad: float32 [1024, 4608], P('dp', 'tensor')
The draws below stay inside these ranges and needn't reach their ends.
All inputs are finite; a program needn't handle non-finite values.
Results may differ from the reference program's by a relative error of at most 0.0095.
Values may be sent and summed in bfloat16 or wider, within the bound.
A program may use at most 256 MiB of HBM per device.

```python
import math
import jax
import jax.numpy as jnp
from jax import lax

D = 1024
FF = 4608
KERNEL = 3
LEN = 1024
TOKENS = 32768


def draw_tokens(key, part):
    key_base, key_rows, key_cols = jax.random.split(key, 3)
    row_scale = 0.4 * jnp.exp(jax.random.uniform(key_rows, (TOKENS, 1), jnp.float32, 0.0, math.log(10.0)))
    col_scale = jnp.exp(jax.random.uniform(key_cols, (1, D), jnp.float32, -0.69, 0.69))
    base_vals = jnp.clip(jax.random.normal(key_base, (TOKENS, D), jnp.float32), -5.0, 5.0)
    return (base_vals * row_scale * col_scale).astype(jnp.bfloat16)


def draw_grad_out(key, part):
    position = lax.broadcasted_iota(jnp.float32, (TOKENS, 1), 0) / TOKENS
    row_scale = 0.6 * jnp.exp(position * math.log(3.0))
    base_vals = jnp.clip(jax.random.normal(key, (TOKENS, D), jnp.float32), -5.0, 5.0)
    return (base_vals * row_scale).astype(jnp.bfloat16)


def steps_of(own_key, extent, cuts, smallest, high):
    level = 1.0
    for dim, shards_of in cuts:
        steps = jax.random.uniform(jax.random.fold_in(jax.random.fold_in(own_key, 6), dim), (shards_of,), jnp.float32, smallest / len(cuts), high / len(cuts))
        level = level * jnp.repeat(jnp.exp(steps), extent[dim] // shards_of).reshape((-1,) + (1,) * (len(extent) - 1 - dim))
    return level


def centred(rng, shape, width, bound, cuts=(), kind=jnp.bfloat16):
    factor_of = steps_of(rng, shape, cuts, -0.22, 0.18) if cuts else 1.0
    array = jax.random.normal(rng, shape, jnp.float32) * width * factor_of
    return jnp.minimum(jnp.maximum(array, -bound), bound).astype(kind)


def setup_inputs(seed: int = 0) -> dict:
    key_of = jax.random.split(jax.random.key(seed), 10)
    return {
        "tokens": draw_tokens(jax.random.fold_in(key_of[9], 71), 0),
        "gain_mix": jnp.clip(1.0 + 0.18 * jax.random.normal(key_of[1], (D,), jnp.float32), 0.1, 1.9),
        "in_weight": centred(key_of[2], (3, D, D), D ** -0.5, 0.1875, ((1, 16), (2, 2))),
        "conv_weight": centred(key_of[3], (KERNEL, D), 0.6, 3.0, (), jnp.float32),
        "out_weight": centred(key_of[4], (D, D), D ** -0.5, 0.1875, ((0, 16), (1, 2))),
        "gain_ff": jnp.clip(1.0 + 0.18 * jax.random.normal(key_of[5], (D,), jnp.float32), 0.1, 1.9),
        "gate_up_weight": centred(key_of[6], (2, D, FF), D ** -0.5, 0.1875, ((1, 16), (2, 2))),
        "down_weight": centred(key_of[7], (D, FF), FF ** -0.5, 0.09375, ((0, 16), (1, 2))),
        "grad_out": draw_grad_out(jax.random.fold_in(key_of[9], 71), 0),
    }


EPS = 1e-05
HIGH = lax.Precision.HIGHEST

@jax.custom_vjp
def low(v):
    return lax.optimization_barrier(v.astype(jnp.bfloat16)).astype(jnp.float32)

@jax.custom_vjp
def low_back(v):
    return v

def low_keep(v):
    return (low(v), None)

def low_pass(kept, grad):
    return (grad,)

def back_keep(v):
    return (v, None)

def back_low(kept, grad):
    return (low(grad),)
low.defvjp(low_keep, low_pass)
low_back.defvjp(back_keep, back_low)

def rms_norm(values, gain_vec):
    return values * lax.rsqrt(lax.optimization_barrier(jnp.mean(values * values, axis=-1, keepdims=True)) + EPS) * gain_vec

def shifted(values, shift_by):
    return jnp.pad(values[:, :values.shape[1] - shift_by], ((0, 0), (shift_by, 0), (0, 0)))

def forward(block_in, gain_mix, in_weight, conv_weight, out_weight, gain_ff, gate_up_weight, down_weight):
    normed_mix = low(rms_norm(block_in, gain_mix))
    projected = low_back(jnp.einsum('nld,jdc->jnlc', normed_mix, in_weight, precision=HIGH))
    mixed_in = projected[0] * projected[2]
    conv_out = conv_weight[0] * shifted(mixed_in, 2) + conv_weight[1] * shifted(mixed_in, 1) + conv_weight[2] * mixed_in
    gated_rows = low(projected[1] * conv_out)
    residual = block_in + low_back(jnp.einsum('nlc,dc->nld', gated_rows, out_weight, precision=HIGH))
    normed_ff = low(rms_norm(residual, gain_ff))
    gate_up = low_back(jnp.einsum('nld,jdf->jnlf', normed_ff, gate_up_weight, precision=HIGH))
    hidden = low(jax.nn.silu(gate_up[0]) * gate_up[1])
    return residual + jnp.einsum('nlf,df->nld', hidden, down_weight, precision=HIGH)

def reference(tokens, gain_mix, in_weight, conv_weight, out_weight, gain_ff, gate_up_weight, down_weight, grad_out):
    weights_f32 = tuple((weight_arg.astype(jnp.float32) for weight_arg in (gain_mix, in_weight, conv_weight, out_weight, gain_ff, gate_up_weight, down_weight)))
    seq_total = TOKENS // LEN
    per_block = math.gcd(seq_total, 4)
    inputs_all = tokens.astype(jnp.float32).reshape(seq_total // per_block, per_block, LEN, D)
    cot_all = grad_out.astype(jnp.float32).reshape(seq_total // per_block, per_block, LEN, D)

    def one_block(totals, block_data):
        block_in, block_cot = block_data
        block_out, pull_back = jax.vjp(forward, block_in, *weights_f32)
        grads_all = pull_back(block_cot)
        totals = tuple((so_far + added for so_far, added in zip(totals, grads_all[1:])))
        return (totals, (block_out, grads_all[0]))
    zero_grads = tuple((jnp.zeros(weight_arg.shape, jnp.float32) for weight_arg in weights_f32))
    totals, (outs_all, input_grads) = lax.scan(one_block, zero_grads, (inputs_all, cot_all))
    block_out = outs_all.reshape(TOKENS, D).astype(jnp.bfloat16)
    input_grad = input_grads.reshape(TOKENS, D)
    return (block_out, input_grad, totals[0], totals[1], totals[2], totals[3], totals[4], totals[5], totals[6])
```

```python
import jax
import jax.numpy as jnp
from jax import lax
from jax.sharding import PartitionSpec as P

LEN = 1024


EPS = 1e-05


def norm_scale(values):
    return lax.rsqrt(jnp.mean(values * values, axis=-1, keepdims=True) + EPS)


def delayed(values, shift_by):
    return jnp.pad(values[:, : values.shape[1] - shift_by], ((0, 0), (shift_by, 0), (0, 0)))


def advanced(values, shift_by):
    return jnp.pad(values[:, shift_by:], ((0, 0), (0, shift_by), (0, 0)))


def norm_back(values, row_scale, gain_vec, grad_normed):
    weighted = grad_normed * gain_vec
    inner_mean = jnp.mean(weighted * values, axis=-1, keepdims=True)
    grad_values = row_scale * weighted - values * row_scale**3 * inner_mean
    gain_grad = jnp.sum(grad_normed * values * row_scale, axis=0)
    return (grad_values, gain_grad)


def gather_cols(shard, col_axis):
    part = lax.all_gather(shard, "tensor", axis=col_axis, tiled=True)
    return lax.all_gather(part, "dp", axis=col_axis - 1, tiled=True)


def scatter_sum(partial, col_axis):
    if col_axis == 2:
        return jnp.stack([scatter_sum(one, 1) for one in partial])
    part = lax.psum_scatter(
        partial.astype(jnp.bfloat16), "dp", scatter_dimension=col_axis - 1, tiled=True
    )
    return lax.psum_scatter(part, "tensor", scatter_dimension=col_axis, tiled=True).astype(
        jnp.float32
    )


def per_device(
    tokens,
    gain_mix,
    in_weight,
    conv_weight,
    out_weight,
    gain_ff,
    gate_up_weight,
    down_weight,
    grad_out,
):
    inputs = tokens.astype(jnp.float32)
    in_full = gather_cols(in_weight, 2)
    out_full = gather_cols(out_weight, 1)
    gate_up_full = gather_cols(gate_up_weight, 2)
    down_full = gather_cols(down_weight, 1)
    rows, width = tokens.shape
    seq_count = rows // LEN
    scale_mix = norm_scale(inputs)
    normed_mix = (inputs * scale_mix * gain_mix).astype(jnp.bfloat16)
    projected = jnp.einsum("gd,jdc->jgc", normed_mix, in_full, preferred_element_type=jnp.float32)
    shaped = (seq_count, LEN, width)
    input_gate = projected[0].reshape(shaped)
    output_gate = projected[1].reshape(shaped)
    value_part = projected[2].reshape(shaped)
    mixed_in = input_gate * value_part
    conv_out = (
        conv_weight[0] * delayed(mixed_in, 2)
        + conv_weight[1] * delayed(mixed_in, 1)
        + conv_weight[2] * mixed_in
    )
    gated_rows = (output_gate * conv_out).astype(jnp.bfloat16).reshape(rows, width)
    residual = inputs + lax.dot_general(
        gated_rows, out_full, (((1,), (1,)), ((), ())), preferred_element_type=jnp.float32
    )
    scale_ff = norm_scale(residual)
    normed_ff = (residual * scale_ff * gain_ff).astype(jnp.bfloat16)
    gate_up = jnp.einsum(
        "gd,jdf->jgf", normed_ff, gate_up_full, preferred_element_type=jnp.float32
    )
    gate_pre = gate_up[0]
    up_value = gate_up[1]
    sigmoid_gate = jax.nn.sigmoid(gate_pre)
    silu_gate = gate_pre * sigmoid_gate
    hidden = (silu_gate * up_value).astype(jnp.bfloat16)
    block_out = (
        residual
        + lax.dot_general(
            hidden, down_full, (((1,), (1,)), ((), ())), preferred_element_type=jnp.float32
        )
    ).astype(jnp.bfloat16)
    hidden_grad = jnp.dot(grad_out, down_full, preferred_element_type=jnp.float32)
    down_grad = lax.dot_general(
        grad_out, hidden, (((0,), (0,)), ((), ())), preferred_element_type=jnp.float32
    )
    down_sum = scatter_sum(down_grad, 1)
    silu_slope = sigmoid_gate * (1.0 + gate_pre * (1.0 - sigmoid_gate))
    gate_grad = (hidden_grad * up_value * silu_slope).astype(jnp.bfloat16)
    up_grad = (hidden_grad * silu_gate).astype(jnp.bfloat16)
    gate_up_grad = jnp.stack([gate_grad, up_grad])
    gate_up_weight_grad = jnp.einsum(
        "gd,jgf->jdf", normed_ff, gate_up_grad, preferred_element_type=jnp.float32
    )
    gate_up_sum = scatter_sum(gate_up_weight_grad, 2)
    ffn_in_grad = jnp.einsum(
        "jgf,jdf->gd", gate_up_grad, gate_up_full, preferred_element_type=jnp.float32
    )
    residual_back, gain_ff_grad = norm_back(residual, scale_ff, gain_ff, ffn_in_grad)
    residual_grad = grad_out.astype(jnp.float32) + residual_back
    mixer_grads = residual_grad.astype(jnp.bfloat16)
    gated_grad = jnp.dot(mixer_grads, out_full, preferred_element_type=jnp.float32).reshape(shaped)
    out_weight_grad = lax.dot_general(
        mixer_grads, gated_rows, (((0,), (0,)), ((), ())), preferred_element_type=jnp.float32
    )
    out_sum = scatter_sum(out_weight_grad, 1)
    output_gate_grad = gated_grad * conv_out
    conv_grad_in = gated_grad * output_gate
    mixed_grad = (
        conv_weight[2] * conv_grad_in
        + conv_weight[1] * advanced(conv_grad_in, 1)
        + conv_weight[0] * advanced(conv_grad_in, 2)
    )
    tap_grads = jnp.stack(
        [
            jnp.sum(conv_grad_in * delayed(mixed_in, 2), axis=(0, 1)),
            jnp.sum(conv_grad_in * delayed(mixed_in, 1), axis=(0, 1)),
            jnp.sum(conv_grad_in * mixed_in, axis=(0, 1)),
        ]
    )
    proj_grad = (
        jnp.stack([mixed_grad * value_part, output_gate_grad, mixed_grad * input_gate])
        .astype(jnp.bfloat16)
        .reshape(3, rows, width)
    )
    in_weight_grad = jnp.einsum(
        "gd,jgc->jdc", normed_mix, proj_grad, preferred_element_type=jnp.float32
    )
    in_sum = scatter_sum(in_weight_grad, 2)
    mixer_in_grad = jnp.einsum(
        "jgc,jdc->gd", proj_grad, in_full, preferred_element_type=jnp.float32
    )
    input_back, gain_mix_grad = norm_back(inputs, scale_mix, gain_mix, mixer_in_grad)
    input_grad = residual_grad + input_back
    gain_mix_sum, gain_ff_sum, conv_sum = lax.psum(
        (gain_mix_grad, gain_ff_grad, tap_grads), ("dp", "tensor")
    )
    return (
        block_out,
        input_grad,
        gain_mix_sum,
        in_sum,
        conv_sum,
        out_sum,
        gain_ff_sum,
        gate_up_sum,
        down_sum,
    )


def solution(mesh):
    in_specs = (
        P(("dp", "tensor"), None),
        P(),
        P(None, "dp", "tensor"),
        P(),
        P("dp", "tensor"),
        P(),
        P(None, "dp", "tensor"),
        P("dp", "tensor"),
        P(("dp", "tensor"), None),
    )
    out_specs = (
        P(("dp", "tensor"), None),
        P(("dp", "tensor"), None),
        P(),
        P(None, "dp", "tensor"),
        P(),
        P("dp", "tensor"),
        P(),
        P(None, "dp", "tensor"),
        P("dp", "tensor"),
    )
    return jax.shard_map(
        per_device, mesh=mesh, in_specs=in_specs, out_specs=out_specs, check_vma=False
    )
```

```python
import functools

import jax
import jax.numpy as jnp
from jax import lax
from jax.experimental import pallas as pl
from jax.experimental.pallas import tpu as pltpu
from jax.sharding import PartitionSpec as P

LEN = 1024


EPS = 1e-05


def norm_scale(values):
    return lax.rsqrt(jnp.mean(values * values, axis=-1, keepdims=True) + EPS)


def delayed(values, shift_by):
    return jnp.pad(values[:, : values.shape[1] - shift_by], ((0, 0), (shift_by, 0), (0, 0)))


def advanced(values, shift_by):
    return jnp.pad(values[:, shift_by:], ((0, 0), (0, shift_by), (0, 0)))


def norm_back(values, row_scale, gain_vec, grad_normed):
    weighted = grad_normed * gain_vec
    inner_mean = jnp.mean(weighted * values, axis=-1, keepdims=True)
    grad_values = row_scale * weighted - values * row_scale**3 * inner_mean
    gain_grad = jnp.sum(grad_normed * values * row_scale, axis=0)
    return (grad_values, gain_grad)


MESH = pl.DeviceIdType.MESH
ORDERS = ("xzy", "yzx", "zxy", "zyx")
GROUPS = ((0, 0, 3), (1, 0, 1), (2, 0, 1), (2, 1, 1), (3, 0, 1))
STAGES = {"x": 0, "y": 1, "z": 2, "c": 3}


class Place:
    def __init__(self, slabs):
        dp = lax.axis_index("dp")
        self.dp, self.x = dp, lax.axis_index("tensor")
        self.slabs = slabs
        self.a = dp // 4
        self.y = (dp // 2) % 2
        self.c = dp % 2
        self.peer = {
            "x": (dp, 1 - self.x),
            "y": (dp + 2 - 4 * self.y, self.x),
            "c": (dp + 1 - 2 * self.c, self.x),
            "down": (dp - 4, self.x),
            "up": (dp + 4, self.x),
        }
        self.has = {"down": self.a > 0, "up": self.a < slabs - 1}

    def greet(self):
        barrier = pltpu.get_barrier_semaphore()
        for name in ("x", "y", "c"):
            pl.semaphore_signal(barrier, 1, device_id=self.peer[name], device_id_type=MESH)
        for name in ("down", "up"):

            @pl.when(self.has[name])
            def _(name=name):
                pl.semaphore_signal(barrier, 1, device_id=self.peer[name], device_id_type=MESH)

        ends = self.has["down"].astype(jnp.int32) + self.has["up"].astype(jnp.int32)
        pl.semaphore_wait(barrier, 3 + ends)


def pick(own, which):
    if which == "all":
        return slice(None)
    return own if which == "own" else 1 - own


def gather_ticks(place, full, planes, rows, cols, order, send_sem, recv_sem, base):
    here = place
    n = cols

    def region(slab, y, c, x):
        columns = slice(None) if x == "all" else pl.ds(pl.multiple_of(pick(here.x, x) * n, 128), n)
        return full.at[planes, slab, pick(here.y, y), pick(here.c, c), rows, columns]

    def span(stage, side):
        i = order.index(stage) if stage != "c" else 3
        done = order[:i]
        sel = {d: ("all" if d in done else "own") for d in "xy"}
        if stage in "xy":
            sel[stage] = side
        return sel["y"], (side if stage == "c" else "own"), sel["x"]

    def copy(stage, slab, side, peer):
        ref = region(slab, *span(stage, side))
        k = STAGES[stage]
        return pltpu.make_async_remote_copy(
            ref, ref, send_sem.at[base, k, slab], recv_sem.at[base, k, slab], peer, MESH
        )

    zi = order.index("z")
    pre, post = order[:zi], order[zi + 1 :] + "c"
    total = len(pre) + here.slabs + len(post) + 1
    ticks = [[] for _ in range(total)]
    sends = []

    def start(stage, slab, peer):
        copy(stage, slab, "own", peer).start()

    def finish(stage, slab):
        copy(stage, slab, "own" if stage == "z" else "other", here.peer["x"]).wait_recv()

    def chain(t, stages, slab, cond):
        for i, stage in enumerate(stages):
            ticks[t + i].append((cond, functools.partial(start, stage, slab, here.peer[stage])))
            ticks[t + i + 1].append((cond, functools.partial(finish, stage, slab)))
            sends.append((cond, stage, slab))

    chain(0, pre, here.a, None)
    t0 = len(pre)
    for name in ("down", "up"):
        ticks[t0].append((here.has[name], functools.partial(start, "z", here.a, here.peer[name])))
        sends.append((here.has[name], "z", here.a))
    chain(t0, post, here.a, None)
    for s in range(1, here.slabs):
        for slab, come, to in (
            (here.a - s, here.a >= s, "up"),
            (here.a + s, here.a + s < here.slabs, "down"),
        ):
            both = jnp.logical_and(come, here.has[to])
            ticks[t0 + s].append((come, functools.partial(finish, "z", slab)))
            ticks[t0 + s].append((both, functools.partial(start, "z", slab, here.peer[to])))
            sends.append((both, "z", slab))
            chain(t0 + s, post, slab, come)

    def drain():
        for cond, stage, slab in sends:
            when(cond, copy(stage, slab, "own", here.peer["x"]).wait_send)

    return ticks, drain


def when(cond, action):
    if cond is None:
        action()
    else:
        pl.when(cond)(action)


def merge(schedules, lag):
    longest = max(lag * i + len(s) for i, s in enumerate(schedules))
    for t in range(longest):
        for i, s in enumerate(schedules):
            k = t - lag * i
            if 0 <= k < len(s):
                for cond, action in s[k]:
                    when(cond, action)


def parts_of(rows):
    return 4 if rows >= 64 else 1


def gather_kernel(slabs, layout, lag, *refs):
    count = len(layout["shapes"])
    shards, fulls = refs[:count], refs[count : 2 * count]
    send_sem, recv_sem, own_sem = refs[2 * count :]
    place = Place(slabs)
    local = []
    for i, (shard, full) in enumerate(zip(shards, fulls)):
        n = shard.shape[2]
        columns = pl.ds(pl.multiple_of(place.x * n, 128), n)
        own = pltpu.make_async_copy(
            shard, full.at[:, place.a, place.y, place.c, :, columns], own_sem.at[i]
        )
        own.start()
        local.append(own)
    place.greet()
    for own in local:
        own.wait()
    schedules, drains = [], []
    base = 0
    for i, plane0, planes in layout["groups"]:
        rows, n = shards[i].shape[1:]
        parts = parts_of(rows)
        size = rows // parts
        both = []
        for p in range(parts):
            ticks, drain = gather_ticks(
                place, fulls[i], pl.ds(plane0, planes), pl.ds(p * size, size), n,
                ORDERS[p], send_sem, recv_sem, base,
            )
            base += 1
            both.append(ticks)
            drains.append(drain)
        length = max(len(t) for t in both)
        schedules.append([sum((t[k] for t in both if k < len(t)), []) for k in range(length)])
    merge(schedules, lag)
    for drain in drains:
        drain()


def gather_all(shards, groups, dp, tensor, lag=2):
    slabs = dp // 4
    shapes = [s.shape for s in shards]
    parts = parts_of(shapes[0][1])
    bases = len(groups) * parts
    out = [
        jax.ShapeDtypeStruct((s[0], slabs, 2, 2, s[1], s[2] * tensor), jnp.bfloat16) for s in shapes
    ]
    full = pl.pallas_call(
        functools.partial(gather_kernel, slabs, {"shapes": shapes, "groups": groups}, lag),
        out_shape=out,
        in_specs=[pl.BlockSpec(memory_space=pltpu.VMEM)] * len(shards),
        out_specs=[pl.BlockSpec(memory_space=pl.ANY)] * len(shards),
        scratch_shapes=[
            pltpu.SemaphoreType.DMA((bases, 4, slabs)),
            pltpu.SemaphoreType.DMA((bases, 4, slabs)),
            pltpu.SemaphoreType.DMA((len(shards),)),
        ],
        compiler_params=pltpu.CompilerParams(collective_id=0, has_side_effects=True),
        name="gather_weights",
    )(*shards)
    return [f.reshape(s[0], dp * s[1], s[2] * tensor) for f, s in zip(full, shapes)]


def scatter_sum(partial, col_axis):
    if col_axis == 2:
        return jnp.stack([scatter_sum(one, 1) for one in partial])
    part = lax.psum_scatter(
        partial.astype(jnp.bfloat16), "dp", scatter_dimension=col_axis - 1, tiled=True
    )
    return lax.psum_scatter(part, "tensor", scatter_dimension=col_axis, tiled=True).astype(
        jnp.float32
    )


def per_device(
    tokens,
    gain_mix,
    in_weight,
    conv_weight,
    out_weight,
    gain_ff,
    gate_up_weight,
    down_weight,
    grad_out,
):
    inputs = tokens.astype(jnp.float32)
    in_full, out_full, gate_up_full, down_full = gather_all(
        [in_weight, out_weight[None], gate_up_weight, down_weight[None]],
        GROUPS,
        lax.axis_size("dp"),
        lax.axis_size("tensor"),
    )
    out_full, down_full = out_full[0], down_full[0]
    rows, width = tokens.shape
    seq_count = rows // LEN
    scale_mix = norm_scale(inputs)
    normed_mix = (inputs * scale_mix * gain_mix).astype(jnp.bfloat16)
    projected = jnp.einsum("gd,jdc->jgc", normed_mix, in_full, preferred_element_type=jnp.float32)
    shaped = (seq_count, LEN, width)
    input_gate = projected[0].reshape(shaped)
    output_gate = projected[1].reshape(shaped)
    value_part = projected[2].reshape(shaped)
    mixed_in = input_gate * value_part
    conv_out = (
        conv_weight[0] * delayed(mixed_in, 2)
        + conv_weight[1] * delayed(mixed_in, 1)
        + conv_weight[2] * mixed_in
    )
    gated_rows = (output_gate * conv_out).astype(jnp.bfloat16).reshape(rows, width)
    residual = inputs + lax.dot_general(
        gated_rows, out_full, (((1,), (1,)), ((), ())), preferred_element_type=jnp.float32
    )
    scale_ff = norm_scale(residual)
    normed_ff = (residual * scale_ff * gain_ff).astype(jnp.bfloat16)
    gate_up = jnp.einsum(
        "gd,jdf->jgf", normed_ff, gate_up_full, preferred_element_type=jnp.float32
    )
    gate_pre = gate_up[0]
    up_value = gate_up[1]
    sigmoid_gate = jax.nn.sigmoid(gate_pre)
    silu_gate = gate_pre * sigmoid_gate
    hidden = (silu_gate * up_value).astype(jnp.bfloat16)
    block_out = (
        residual
        + lax.dot_general(
            hidden, down_full, (((1,), (1,)), ((), ())), preferred_element_type=jnp.float32
        )
    ).astype(jnp.bfloat16)
    hidden_grad = jnp.dot(grad_out, down_full, preferred_element_type=jnp.float32)
    down_grad = lax.dot_general(
        grad_out, hidden, (((0,), (0,)), ((), ())), preferred_element_type=jnp.float32
    )
    down_sum = scatter_sum(down_grad, 1)
    silu_slope = sigmoid_gate * (1.0 + gate_pre * (1.0 - sigmoid_gate))
    gate_grad = (hidden_grad * up_value * silu_slope).astype(jnp.bfloat16)
    up_grad = (hidden_grad * silu_gate).astype(jnp.bfloat16)
    gate_up_grad = jnp.stack([gate_grad, up_grad])
    gate_up_weight_grad = jnp.einsum(
        "gd,jgf->jdf", normed_ff, gate_up_grad, preferred_element_type=jnp.float32
    )
    gate_up_sum = scatter_sum(gate_up_weight_grad, 2)
    ffn_in_grad = jnp.einsum(
        "jgf,jdf->gd", gate_up_grad, gate_up_full, preferred_element_type=jnp.float32
    )
    residual_back, gain_ff_grad = norm_back(residual, scale_ff, gain_ff, ffn_in_grad)
    residual_grad = grad_out.astype(jnp.float32) + residual_back
    mixer_grads = residual_grad.astype(jnp.bfloat16)
    gated_grad = jnp.dot(mixer_grads, out_full, preferred_element_type=jnp.float32).reshape(shaped)
    out_weight_grad = lax.dot_general(
        mixer_grads, gated_rows, (((0,), (0,)), ((), ())), preferred_element_type=jnp.float32
    )
    out_sum = scatter_sum(out_weight_grad, 1)
    output_gate_grad = gated_grad * conv_out
    conv_grad_in = gated_grad * output_gate
    mixed_grad = (
        conv_weight[2] * conv_grad_in
        + conv_weight[1] * advanced(conv_grad_in, 1)
        + conv_weight[0] * advanced(conv_grad_in, 2)
    )
    tap_grads = jnp.stack(
        [
            jnp.sum(conv_grad_in * delayed(mixed_in, 2), axis=(0, 1)),
            jnp.sum(conv_grad_in * delayed(mixed_in, 1), axis=(0, 1)),
            jnp.sum(conv_grad_in * mixed_in, axis=(0, 1)),
        ]
    )
    proj_grad = (
        jnp.stack([mixed_grad * value_part, output_gate_grad, mixed_grad * input_gate])
        .astype(jnp.bfloat16)
        .reshape(3, rows, width)
    )
    in_weight_grad = jnp.einsum(
        "gd,jgc->jdc", normed_mix, proj_grad, preferred_element_type=jnp.float32
    )
    in_sum = scatter_sum(in_weight_grad, 2)
    mixer_in_grad = jnp.einsum(
        "jgc,jdc->gd", proj_grad, in_full, preferred_element_type=jnp.float32
    )
    input_back, gain_mix_grad = norm_back(inputs, scale_mix, gain_mix, mixer_in_grad)
    input_grad = residual_grad + input_back
    gain_mix_sum, gain_ff_sum, conv_sum = lax.psum(
        (gain_mix_grad, gain_ff_grad, tap_grads), ("dp", "tensor")
    )
    return (
        block_out,
        input_grad,
        gain_mix_sum,
        in_sum,
        conv_sum,
        out_sum,
        gain_ff_sum,
        gate_up_sum,
        down_sum,
    )


def solution(mesh):
    in_specs = (
        P(("dp", "tensor"), None),
        P(),
        P(None, "dp", "tensor"),
        P(),
        P("dp", "tensor"),
        P(),
        P(None, "dp", "tensor"),
        P("dp", "tensor"),
        P(("dp", "tensor"), None),
    )
    out_specs = (
        P(("dp", "tensor"), None),
        P(("dp", "tensor"), None),
        P(),
        P(None, "dp", "tensor"),
        P(),
        P("dp", "tensor"),
        P(),
        P(None, "dp", "tensor"),
        P("dp", "tensor"),
    )
    return jax.shard_map(
        per_device, mesh=mesh, in_specs=in_specs, out_specs=out_specs, check_vma=False
    )
```

```python
import functools

import jax
import jax.numpy as jnp
from jax import lax
from jax.experimental import pallas as pl
from jax.experimental.pallas import tpu as pltpu
from jax.sharding import PartitionSpec as P

LEN = 1024


EPS = 1e-05


def norm_scale(values):
    return lax.rsqrt(jnp.mean(values * values, axis=-1, keepdims=True) + EPS)


def delayed(values, shift_by):
    return jnp.pad(values[:, : values.shape[1] - shift_by], ((0, 0), (shift_by, 0), (0, 0)))


def advanced(values, shift_by):
    return jnp.pad(values[:, shift_by:], ((0, 0), (0, shift_by), (0, 0)))


def norm_back(values, row_scale, gain_vec, grad_normed):
    weighted = grad_normed * gain_vec
    inner_mean = jnp.mean(weighted * values, axis=-1, keepdims=True)
    grad_values = row_scale * weighted - values * row_scale**3 * inner_mean
    gain_grad = jnp.sum(grad_normed * values * row_scale, axis=0)
    return (grad_values, gain_grad)


MESH = pl.DeviceIdType.MESH
ORDERS = ("xzy", "yzx", "zxy", "zyx")
GROUPS = ((0, 0, 3), (1, 0, 1), (2, 0, 1), (2, 1, 1), (3, 0, 1))
SUM_GROUPS = ((0, 0, 1), (1, 0, 1), (1, 1, 1), (2, 0, 3), (3, 0, 1))
STAGES = {"x": 0, "y": 1, "z": 2, "c": 3}


class Place:
    def __init__(self, slabs):
        dp = lax.axis_index("dp")
        self.dp, self.x = dp, lax.axis_index("tensor")
        self.slabs = slabs
        self.a = dp // 4
        self.y = (dp // 2) % 2
        self.c = dp % 2
        self.peer = {
            "x": (dp, 1 - self.x),
            "y": (dp + 2 - 4 * self.y, self.x),
            "c": (dp + 1 - 2 * self.c, self.x),
            "down": (dp - 4, self.x),
            "up": (dp + 4, self.x),
        }
        self.has = {"down": self.a > 0, "up": self.a < slabs - 1}

    def greet(self, chain=False):
        barrier = pltpu.get_barrier_semaphore()
        for name in ("x", "y", "c"):
            pl.semaphore_signal(barrier, 1, device_id=self.peer[name], device_id_type=MESH)
        if chain:
            for slab in range(self.slabs):

                @pl.when(slab != self.a)
                def _(slab=slab):
                    pl.semaphore_signal(
                        barrier,
                        1,
                        device_id=(self.dp + 4 * (slab - self.a), self.x),
                        device_id_type=MESH,
                    )

            pl.semaphore_wait(barrier, 2 + self.slabs)
            return
        for name in ("down", "up"):

            @pl.when(self.has[name])
            def _(name=name):
                pl.semaphore_signal(barrier, 1, device_id=self.peer[name], device_id_type=MESH)

        ends = self.has["down"].astype(jnp.int32) + self.has["up"].astype(jnp.int32)
        pl.semaphore_wait(barrier, 3 + ends)


def pick(own, which):
    if which == "all":
        return slice(None)
    return own if which == "own" else 1 - own


def gather_ticks(place, full, planes, rows, cols, order, send_sem, recv_sem, base):
    here = place
    n = cols

    def region(slab, y, c, x):
        columns = slice(None) if x == "all" else pl.ds(pl.multiple_of(pick(here.x, x) * n, 128), n)
        return full.at[planes, slab, pick(here.y, y), pick(here.c, c), rows, columns]

    def span(stage, side):
        i = order.index(stage) if stage != "c" else 3
        done = order[:i]
        sel = {d: ("all" if d in done else "own") for d in "xy"}
        if stage in "xy":
            sel[stage] = side
        return sel["y"], (side if stage == "c" else "own"), sel["x"]

    def copy(stage, slab, side, peer):
        ref = region(slab, *span(stage, side))
        k = STAGES[stage]
        return pltpu.make_async_remote_copy(
            ref, ref, send_sem.at[base, k, slab], recv_sem.at[base, k, slab], peer, MESH
        )

    zi = order.index("z")
    pre, post = order[:zi], order[zi + 1 :] + "c"
    total = len(pre) + here.slabs + len(post) + 1
    ticks = [[] for _ in range(total)]
    sends = []

    def start(stage, slab, peer):
        copy(stage, slab, "own", peer).start()

    def finish(stage, slab):
        copy(stage, slab, "own" if stage == "z" else "other", here.peer["x"]).wait_recv()

    def chain(t, stages, slab, cond):
        for i, stage in enumerate(stages):
            ticks[t + i].append((cond, functools.partial(start, stage, slab, here.peer[stage])))
            ticks[t + i + 1].append((cond, functools.partial(finish, stage, slab)))
            sends.append((cond, stage, slab))

    chain(0, pre, here.a, None)
    t0 = len(pre)
    for name in ("down", "up"):
        ticks[t0].append((here.has[name], functools.partial(start, "z", here.a, here.peer[name])))
        sends.append((here.has[name], "z", here.a))
    chain(t0, post, here.a, None)
    for s in range(1, here.slabs):
        for slab, come, to in (
            (here.a - s, here.a >= s, "up"),
            (here.a + s, here.a + s < here.slabs, "down"),
        ):
            both = jnp.logical_and(come, here.has[to])
            ticks[t0 + s].append((come, functools.partial(finish, "z", slab)))
            ticks[t0 + s].append((both, functools.partial(start, "z", slab, here.peer[to])))
            sends.append((both, "z", slab))
            chain(t0 + s, post, slab, come)

    def drain():
        for cond, stage, slab in sends:
            when(cond, copy(stage, slab, "own", here.peer["x"]).wait_send)

    return ticks, drain


def when(cond, action):
    if cond is None:
        action()
    else:
        pl.when(cond)(action)


def merge(schedules, lag):
    longest = max(lag * i + len(s) for i, s in enumerate(schedules))
    for t in range(longest):
        for i, s in enumerate(schedules):
            k = t - lag * i
            if 0 <= k < len(s):
                for cond, action in s[k]:
                    when(cond, action)


def parts_of(rows):
    return 4 if rows >= 64 else 1


def gather_kernel(slabs, layout, lag, *refs):
    count = len(layout["shapes"])
    shards, fulls = refs[:count], refs[count : 2 * count]
    send_sem, recv_sem, own_sem = refs[2 * count :]
    place = Place(slabs)
    local = []
    for i, (shard, full) in enumerate(zip(shards, fulls)):
        n = shard.shape[2]
        columns = pl.ds(pl.multiple_of(place.x * n, 128), n)
        own = pltpu.make_async_copy(
            shard, full.at[:, place.a, place.y, place.c, :, columns], own_sem.at[i]
        )
        own.start()
        local.append(own)
    place.greet()
    for own in local:
        own.wait()
    schedules, drains = [], []
    base = 0
    for i, plane0, planes in layout["groups"]:
        rows, n = shards[i].shape[1:]
        parts = parts_of(rows)
        size = rows // parts
        both = []
        for p in range(parts):
            ticks, drain = gather_ticks(
                place, fulls[i], pl.ds(plane0, planes), pl.ds(p * size, size), n,
                ORDERS[p], send_sem, recv_sem, base,
            )
            base += 1
            both.append(ticks)
            drains.append(drain)
        length = max(len(t) for t in both)
        schedules.append([sum((t[k] for t in both if k < len(t)), []) for k in range(length)])
    merge(schedules, lag)
    for drain in drains:
        drain()


def gather_all(shards, groups, dp, tensor, lag=2):
    slabs = dp // 4
    shapes = [s.shape for s in shards]
    parts = parts_of(shapes[0][1])
    bases = len(groups) * parts
    out = [
        jax.ShapeDtypeStruct((s[0], slabs, 2, 2, s[1], s[2] * tensor), jnp.bfloat16) for s in shapes
    ]
    full = pl.pallas_call(
        functools.partial(gather_kernel, slabs, {"shapes": shapes, "groups": groups}, lag),
        out_shape=out,
        in_specs=[pl.BlockSpec(memory_space=pltpu.VMEM)] * len(shards),
        out_specs=[pl.BlockSpec(memory_space=pl.ANY)] * len(shards),
        scratch_shapes=[
            pltpu.SemaphoreType.DMA((bases, 4, slabs)),
            pltpu.SemaphoreType.DMA((bases, 4, slabs)),
            pltpu.SemaphoreType.DMA((len(shards),)),
        ],
        compiler_params=pltpu.CompilerParams(collective_id=0, has_side_effects=True),
        name="gather_weights",
    )(*shards)
    return [f.reshape(s[0], dp * s[1], s[2] * tensor) for f, s in zip(full, shapes)]


def add_into(target, extra):
    rows, cols = target.shape[-2:]
    step = next(w for w in (1152, 1024, 512, 256, 128) if cols % w == 0)
    lead = target.shape[:-2]
    count = 1
    for d in lead:
        count *= d

    def body(i, carry):
        at = []
        k = i // (cols // step)
        for d in reversed(lead):
            at.insert(0, k % d)
            k = k // d
        where = (*at, slice(None), pl.ds(pl.multiple_of((i % (cols // step)) * step, 128), step))
        total = target[where].astype(jnp.float32) + extra[where].astype(jnp.float32)
        target[where] = total.astype(target.dtype)
        return carry

    lax.fori_loop(0, count * (cols // step), body, 0)


class PartSum:
    def __init__(self, place, src, out, planes, rows, n, order, bufs, sems, base):
        self.place, self.src, self.out = place, src, out
        self.planes, self.rows, self.n, self.order = planes, rows, n, order
        self.acc, self.got = bufs["acc"], bufs
        self.load_sem, self.send_sem, self.recv_sem = sems
        self.base = base
        self.sends = []

    def cut(self, ref, slab, y, x):
        place = self.place
        y = slice(None) if y == "all" else pl.ds(pick(place.y, y), 1)
        n = self.n
        x = slice(None) if x == "all" else pl.ds(pl.multiple_of(pick(place.x, x) * n, 128), n)
        return ref.at[:, slab, y, :, x]

    def span(self, stage, side):
        i = self.order.index(stage)
        sel = {d: ("all" if d in self.order[:i] else "own") for d in "xy"}
        if stage in "xy":
            sel[stage] = side
        return sel["y"], sel["x"]

    def load(self, slab):
        return pltpu.make_async_copy(
            self.src.at[self.planes, slab, :, self.place.c, self.rows, :],
            self.acc.at[:, slab],
            self.load_sem.at[self.base, slab],
        )

    def copy(self, stage, slab, peer, slot=None):
        k = STAGES[stage]
        slot = slab if slot is None else slot
        if stage == "c":
            ref = self.src.at[self.planes, slab, :, 1 - self.place.c, self.rows, :]
        else:
            ref = self.cut(self.acc, slab, *self.span(stage, "other"))
        into = self.got[stage]
        into = into.at[:, 0] if (stage != "c" and "z" in self.order[self.order.index(stage) :][1:]) else into.at[:, slot]
        return pltpu.make_async_remote_copy(
            ref, into, self.send_sem.at[self.base, k, slot], self.recv_sem.at[self.base, k, slot],
            peer, MESH,
        )

    def start(self, stage, slab):
        self.copy(stage, slab, self.place.peer[stage]).start()

    def begin(self, slab):
        self.load(slab).start()
        self.start("c", slab)

    def take(self, stage, slab, slot=None):
        copy = self.copy(stage, slab, self.place.peer["x"], slot)
        copy.wait_recv()
        slot = slab if slot is None else slot
        if stage == "c":
            self.load(slab).wait()
            add_into(self.acc.at[:, slab], self.got["c"].at[:, slot])
            return
        first = "z" in self.order[self.order.index(stage) :][1:]
        add_into(
            self.cut(self.acc, slab, *self.span(stage, "own")),
            self.got[stage].at[:, 0 if first else slot],
        )

    def take_z(self, slab, slot):
        self.take("z", slab, slot)

    def send_z(self, slab, to):
        place = self.place
        target = place.a + (1 if to == "up" else -1)
        slot = slab if to == "up" else jnp.where(slab == target, place.slabs, slab)
        self.copy("z", slab, place.peer[to], slot).start()

    def finish(self):
        place = self.place
        y, x = "own", "own"
        rows = self.rows
        self.out[:, rows, :] = self.cut(self.acc, place.a, y, x)[:, 0].astype(jnp.float32)

    def ticks(self):
        place, order = self.place, self.order
        zi = order.index("z")
        after = "c" + "".join(reversed(order[zi + 1 :]))
        before = "".join(reversed(order[:zi]))
        slabs = place.slabs
        ticks = [[] for _ in range(slabs + len(after) + len(before) + 2)]
        bind = functools.partial

        def early(t, slab, cond):
            ticks[t].append((cond, bind(self.begin, slab)))
            self.sends.append((cond, "c", slab, None))
            for i, stage in enumerate(after):
                ticks[t + i + 1].append((cond, bind(self.take, stage, slab)))
                if i + 1 < len(after):
                    ticks[t + i + 1].append((cond, bind(self.start, after[i + 1], slab)))
                    self.sends.append((cond, after[i + 1], slab, None))

        z0 = len(after)
        for k, s in enumerate(range(slabs - 1, 0, -1)):
            for slab, cond, to, more in (
                (place.a + s, place.a + s < slabs, "up", place.has["down"]),
                (place.a - s, place.a >= s, "down", place.has["up"]),
            ):
                early(k, slab, cond)
                both = jnp.logical_and(cond, more)
                ticks[z0 + k].append((both, bind(self.take_z, slab, slab)))
                ticks[z0 + k].append((cond, bind(self.send_z, slab, to)))
                self.sends.append((cond, "z", slab, to))
        last = slabs - 1
        early(last, place.a, None)
        ticks[z0 + last].append((place.has["down"], bind(self.take_z, place.a, place.a)))
        ticks[z0 + last].append((place.has["up"], bind(self.take_z, place.a, slabs)))
        t = z0 + last
        for stage in before:
            ticks[t].append((None, bind(self.start, stage, place.a)))
            self.sends.append((None, stage, place.a, None))
            ticks[t + 1].append((None, bind(self.take, stage, place.a)))
            t += 1
        ticks[t].append((None, self.finish))
        return ticks

    def drain(self):
        place = self.place
        for cond, stage, slab, to in self.sends:
            slot = None
            if to == "down":
                slot = jnp.where(slab == place.a - 1, place.slabs, slab)
            when(cond, self.copy(stage, slab, place.peer["x"], slot).wait_send)


def sum_buffers(planes, slabs, size, n, tensor, order):
    cols = n * tensor
    shapes = {"acc": (planes, slabs, 2, size, cols), "c": (planes, slabs, 2, size, cols)}
    for i, d in enumerate(order):
        ys = 2 if "y" in order[:i] else 1
        xs = cols if "x" in order[:i] else n
        count = slabs + 1 if d == "z" else (1 if "z" in order[i + 1 :] else slabs)
        shapes[d] = (planes, count, ys, size, xs)
    return shapes


def small_sum(place, mine, total, got, sems):
    send_sem, recv_sem = sems
    steps = []

    def exchange(k, name):
        return pltpu.make_async_remote_copy(
            total, got.at[k], send_sem.at[k], recv_sem.at[k], place.peer[name], MESH
        )

    def open_(k, name):
        exchange(k, name).start()

    def close(k, name):
        copy = exchange(k, name)
        copy.wait_send()
        copy.wait_recv()
        total[...] = total[...] + got[k]

    def begin():
        total[...] = mine[...]

    def chain(slab):
        return pltpu.make_async_remote_copy(
            total, got.at[3 + place.a], send_sem.at[3 + slab], recv_sem.at[3 + place.a],
            (place.dp + 4 * (slab - place.a), place.x), MESH,
        )

    def arrival(slab):
        return pltpu.make_async_remote_copy(
            total, got.at[3 + slab], send_sem.at[3 + slab], recv_sem.at[3 + slab],
            (place.dp, place.x), MESH,
        )

    def spread():
        for slab in range(place.slabs):
            pl.when(slab != place.a)(lambda slab=slab: chain(slab).start())

    def collect():
        for slab in range(place.slabs):

            def wait(slab=slab):
                chain(slab).wait_send()
                arrival(slab).wait_recv()

            pl.when(slab != place.a)(wait)
        got[3 + place.a] = total[...]
        value = got[3]
        for slab in range(1, place.slabs):
            value = value + got[3 + slab]
        total[...] = value

    names = "cxy"
    steps.append([begin, functools.partial(open_, 0, "c")])
    for k, name in enumerate(names):
        then = functools.partial(open_, k + 1, names[k + 1]) if k < 2 else spread
        steps.append([functools.partial(close, k, name), then])
    steps.append([collect])
    return [[(None, action) for action in step] for step in steps]


def sum_kernel(slabs, tensor, groups, lag, count, *refs):
    parts_in, small = refs[:count], refs[count]
    outs, small_out = refs[count + 1 : 2 * count + 1], refs[2 * count + 1]
    scratch = list(refs[2 * count + 2 :])
    load_sem, send_sem, recv_sem, small_got, small_send, small_recv = scratch[:6]
    scratch = scratch[6:]
    place = Place(slabs)
    place.greet(chain=True)
    schedules, jobs, base = [], [], 0
    for i, plane0, planes in groups:
        rows, n = outs[i].shape[1:]
        parts = parts_of(rows)
        size = rows // parts
        both = []
        for p in range(parts):
            names = sum_buffers(planes, slabs, size, n, tensor, ORDERS[p])
            bufs = {name: scratch.pop(0) for name in names}
            job = PartSum(
                place, parts_in[i], outs[i].at[pl.ds(plane0, planes)],
                pl.ds(plane0, planes), pl.ds(p * size, size), n, ORDERS[p], bufs,
                (load_sem, send_sem, recv_sem), base,
            )
            base += 1
            both.append(job.ticks())
            jobs.append(job)
        length = max(len(t) for t in both)
        schedules.append([sum((t[k] for t in both if k < len(t)), []) for k in range(length)])
    schedules.append(small_sum(place, small, small_out, small_got, (small_send, small_recv)))
    merge(schedules, lag)
    for job in jobs:
        job.drain()


def sum_all(partials, small, groups, dp, tensor, lag=2):
    slabs = dp // 4
    wide, outs = [], []
    for part in partials:
        planes, rows, cols = part.shape
        wide.append(part.reshape(planes, slabs, 2, 2, rows // dp, cols))
        outs.append(jax.ShapeDtypeStruct((planes, rows // dp, cols // tensor), jnp.float32))
    scratch, bases = [], 0
    for i, _, planes in groups:
        rows, n = outs[i].shape[1:]
        parts = parts_of(rows)
        for p in range(parts):
            shapes = sum_buffers(planes, slabs, rows // parts, n, tensor, ORDERS[p])
            scratch += [pltpu.VMEM(shape, jnp.bfloat16) for shape in shapes.values()]
            bases += 1
    dma = pltpu.SemaphoreType.DMA
    vmem = pl.BlockSpec(memory_space=pltpu.VMEM)
    return pl.pallas_call(
        functools.partial(sum_kernel, slabs, tensor, groups, lag, len(partials)),
        out_shape=[*outs, jax.ShapeDtypeStruct(small.shape, jnp.float32)],
        in_specs=[pl.BlockSpec(memory_space=pl.ANY)] * len(partials) + [vmem],
        out_specs=[vmem] * (len(partials) + 1),
        scratch_shapes=[
            dma((bases, slabs)),
            dma((bases, 4, slabs + 1)),
            dma((bases, 4, slabs + 1)),
            pltpu.VMEM((3 + slabs, *small.shape), jnp.float32),
            dma((3 + slabs,)),
            dma((3 + slabs,)),
            *scratch,
        ],
        compiler_params=pltpu.CompilerParams(
            collective_id=1, has_side_effects=True, vmem_limit_bytes=67043328
        ),
        name="sum_gradients",
    )(*wide, small)


def per_device(
    tokens,
    gain_mix,
    in_weight,
    conv_weight,
    out_weight,
    gain_ff,
    gate_up_weight,
    down_weight,
    grad_out,
):
    inputs = tokens.astype(jnp.float32)
    dp, tensor = lax.axis_size("dp"), lax.axis_size("tensor")
    in_full, out_full, gate_up_full, down_full = gather_all(
        [in_weight, out_weight[None], gate_up_weight, down_weight[None]], GROUPS, dp, tensor
    )
    out_full, down_full = out_full[0], down_full[0]
    rows, width = tokens.shape
    seq_count = rows // LEN
    scale_mix = norm_scale(inputs)
    normed_mix = (inputs * scale_mix * gain_mix).astype(jnp.bfloat16)
    projected = jnp.einsum("gd,jdc->jgc", normed_mix, in_full, preferred_element_type=jnp.float32)
    shaped = (seq_count, LEN, width)
    input_gate = projected[0].reshape(shaped)
    output_gate = projected[1].reshape(shaped)
    value_part = projected[2].reshape(shaped)
    mixed_in = input_gate * value_part
    conv_out = (
        conv_weight[0] * delayed(mixed_in, 2)
        + conv_weight[1] * delayed(mixed_in, 1)
        + conv_weight[2] * mixed_in
    )
    gated_rows = (output_gate * conv_out).astype(jnp.bfloat16).reshape(rows, width)
    residual = inputs + lax.dot_general(
        gated_rows, out_full, (((1,), (1,)), ((), ())), preferred_element_type=jnp.float32
    )
    scale_ff = norm_scale(residual)
    normed_ff = (residual * scale_ff * gain_ff).astype(jnp.bfloat16)
    gate_up = jnp.einsum(
        "gd,jdf->jgf", normed_ff, gate_up_full, preferred_element_type=jnp.float32
    )
    gate_pre = gate_up[0]
    up_value = gate_up[1]
    sigmoid_gate = jax.nn.sigmoid(gate_pre)
    silu_gate = gate_pre * sigmoid_gate
    hidden = (silu_gate * up_value).astype(jnp.bfloat16)
    block_out = (
        residual
        + lax.dot_general(
            hidden, down_full, (((1,), (1,)), ((), ())), preferred_element_type=jnp.float32
        )
    ).astype(jnp.bfloat16)
    hidden_grad = jnp.dot(grad_out, down_full, preferred_element_type=jnp.float32)
    down_grad = lax.dot_general(
        grad_out, hidden, (((0,), (0,)), ((), ())), preferred_element_type=jnp.float32
    )
    silu_slope = sigmoid_gate * (1.0 + gate_pre * (1.0 - sigmoid_gate))
    gate_grad = (hidden_grad * up_value * silu_slope).astype(jnp.bfloat16)
    up_grad = (hidden_grad * silu_gate).astype(jnp.bfloat16)
    gate_up_grad = jnp.stack([gate_grad, up_grad])
    gate_up_weight_grad = jnp.einsum(
        "gd,jgf->jdf", normed_ff, gate_up_grad, preferred_element_type=jnp.float32
    )
    ffn_in_grad = jnp.einsum(
        "jgf,jdf->gd", gate_up_grad, gate_up_full, preferred_element_type=jnp.float32
    )
    residual_back, gain_ff_grad = norm_back(residual, scale_ff, gain_ff, ffn_in_grad)
    residual_grad = grad_out.astype(jnp.float32) + residual_back
    mixer_grads = residual_grad.astype(jnp.bfloat16)
    gated_grad = jnp.dot(mixer_grads, out_full, preferred_element_type=jnp.float32).reshape(shaped)
    out_weight_grad = lax.dot_general(
        mixer_grads, gated_rows, (((0,), (0,)), ((), ())), preferred_element_type=jnp.float32
    )
    output_gate_grad = gated_grad * conv_out
    conv_grad_in = gated_grad * output_gate
    mixed_grad = (
        conv_weight[2] * conv_grad_in
        + conv_weight[1] * advanced(conv_grad_in, 1)
        + conv_weight[0] * advanced(conv_grad_in, 2)
    )
    tap_grads = jnp.stack(
        [
            jnp.sum(conv_grad_in * delayed(mixed_in, 2), axis=(0, 1)),
            jnp.sum(conv_grad_in * delayed(mixed_in, 1), axis=(0, 1)),
            jnp.sum(conv_grad_in * mixed_in, axis=(0, 1)),
        ]
    )
    proj_grad = (
        jnp.stack([mixed_grad * value_part, output_gate_grad, mixed_grad * input_gate])
        .astype(jnp.bfloat16)
        .reshape(3, rows, width)
    )
    in_weight_grad = jnp.einsum(
        "gd,jgc->jdc", normed_mix, proj_grad, preferred_element_type=jnp.float32
    )
    mixer_in_grad = jnp.einsum(
        "jgc,jdc->gd", proj_grad, in_full, preferred_element_type=jnp.float32
    )
    input_back, gain_mix_grad = norm_back(inputs, scale_mix, gain_mix, mixer_in_grad)
    input_grad = residual_grad + input_back
    small = jnp.concatenate(
        [gain_mix_grad[None], gain_ff_grad[None], tap_grads, jnp.zeros((3, width), jnp.float32)]
    )
    down_sum, gate_up_sum, in_sum, out_sum, small_sums = sum_all(
        [
            down_grad.astype(jnp.bfloat16)[None],
            gate_up_weight_grad.astype(jnp.bfloat16),
            in_weight_grad.astype(jnp.bfloat16),
            out_weight_grad.astype(jnp.bfloat16)[None],
        ],
        small,
        SUM_GROUPS,
        dp,
        tensor,
    )
    return (
        block_out,
        input_grad,
        small_sums[0],
        in_sum,
        small_sums[2:5],
        out_sum[0],
        small_sums[1],
        gate_up_sum,
        down_sum[0],
    )


def solution(mesh):
    in_specs = (
        P(("dp", "tensor"), None),
        P(),
        P(None, "dp", "tensor"),
        P(),
        P("dp", "tensor"),
        P(),
        P(None, "dp", "tensor"),
        P("dp", "tensor"),
        P(("dp", "tensor"), None),
    )
    out_specs = (
        P(("dp", "tensor"), None),
        P(("dp", "tensor"), None),
        P(),
        P(None, "dp", "tensor"),
        P(),
        P("dp", "tensor"),
        P(),
        P(None, "dp", "tensor"),
        P("dp", "tensor"),
    )
    return jax.shard_map(
        per_device, mesh=mesh, in_specs=in_specs, out_specs=out_specs, check_vma=False
    )
```

```python
import functools

import jax
import jax.numpy as jnp
from jax import lax
from jax.experimental import pallas as pl
from jax.experimental.pallas import tpu as pltpu
from jax.sharding import PartitionSpec as P

LEN = 1024


EPS = 1e-05


def norm_scale(values):
    return lax.rsqrt(jnp.mean(values * values, axis=-1, keepdims=True) + EPS)


def delayed(values, shift_by):
    return jnp.pad(values[:, : values.shape[1] - shift_by], ((0, 0), (shift_by, 0), (0, 0)))


def advanced(values, shift_by):
    return jnp.pad(values[:, shift_by:], ((0, 0), (0, shift_by), (0, 0)))


def norm_back(values, row_scale, gain_vec, grad_normed):
    weighted = grad_normed * gain_vec
    inner_mean = jnp.mean(weighted * values, axis=-1, keepdims=True)
    grad_values = row_scale * weighted - values * row_scale**3 * inner_mean
    gain_grad = jnp.sum(grad_normed * values * row_scale, axis=0)
    return (grad_values, gain_grad)


MESH = pl.DeviceIdType.MESH
ORDERS = ("xzy", "yzx", "zxy", "zyx")
GROUPS = ((0, 0, 3), (1, 0, 1), (2, 0, 1), (2, 1, 1), (3, 0, 1))
SUM_GROUPS = ((0, 0, 1), (1, 0, 1), (1, 1, 1), (2, 0, 3), (3, 0, 1))
PRODUCTS = ((0, 0, 0, 0), (1, 1, 1, 0), (1, 2, 1, 1), (2, 3, 2, 0), (3, 4, 3, 0))
STAGES = {"x": 0, "y": 1, "z": 2, "c": 3}


class Place:
    def __init__(self, slabs):
        dp = lax.axis_index("dp")
        self.dp, self.x = dp, lax.axis_index("tensor")
        self.slabs = slabs
        self.a = dp // 4
        self.y = (dp // 2) % 2
        self.c = dp % 2
        self.peer = {
            "x": (dp, 1 - self.x),
            "y": (dp + 2 - 4 * self.y, self.x),
            "c": (dp + 1 - 2 * self.c, self.x),
            "down": (dp - 4, self.x),
            "up": (dp + 4, self.x),
        }
        self.has = {"down": self.a > 0, "up": self.a < slabs - 1}

    def greet(self, chain=False):
        barrier = pltpu.get_barrier_semaphore()
        for name in ("x", "y", "c"):
            pl.semaphore_signal(barrier, 1, device_id=self.peer[name], device_id_type=MESH)
        if chain:
            for slab in range(self.slabs):

                @pl.when(slab != self.a)
                def _(slab=slab):
                    pl.semaphore_signal(
                        barrier,
                        1,
                        device_id=(self.dp + 4 * (slab - self.a), self.x),
                        device_id_type=MESH,
                    )

            pl.semaphore_wait(barrier, 2 + self.slabs)
            return
        for name in ("down", "up"):

            @pl.when(self.has[name])
            def _(name=name):
                pl.semaphore_signal(barrier, 1, device_id=self.peer[name], device_id_type=MESH)

        ends = self.has["down"].astype(jnp.int32) + self.has["up"].astype(jnp.int32)
        pl.semaphore_wait(barrier, 3 + ends)


def pick(own, which):
    if which == "all":
        return slice(None)
    return own if which == "own" else 1 - own


def gather_ticks(place, full, planes, rows, cols, order, send_sem, recv_sem, base):
    here = place
    n = cols

    def region(slab, y, c, x):
        columns = slice(None) if x == "all" else pl.ds(pl.multiple_of(pick(here.x, x) * n, 128), n)
        return full.at[planes, slab, pick(here.y, y), pick(here.c, c), rows, columns]

    def span(stage, side):
        i = order.index(stage) if stage != "c" else 3
        done = order[:i]
        sel = {d: ("all" if d in done else "own") for d in "xy"}
        if stage in "xy":
            sel[stage] = side
        return sel["y"], (side if stage == "c" else "own"), sel["x"]

    def copy(stage, slab, side, peer):
        ref = region(slab, *span(stage, side))
        k = STAGES[stage]
        return pltpu.make_async_remote_copy(
            ref, ref, send_sem.at[base, k, slab], recv_sem.at[base, k, slab], peer, MESH
        )

    zi = order.index("z")
    pre, post = order[:zi], order[zi + 1 :] + "c"
    total = len(pre) + here.slabs + len(post) + 1
    ticks = [[] for _ in range(total)]
    sends = []

    def start(stage, slab, peer):
        copy(stage, slab, "own", peer).start()

    def finish(stage, slab):
        copy(stage, slab, "own" if stage == "z" else "other", here.peer["x"]).wait_recv()

    def chain(t, stages, slab, cond):
        for i, stage in enumerate(stages):
            ticks[t + i].append((cond, functools.partial(start, stage, slab, here.peer[stage])))
            ticks[t + i + 1].append((cond, functools.partial(finish, stage, slab)))
            sends.append((cond, stage, slab))

    chain(0, pre, here.a, None)
    t0 = len(pre)
    for name in ("down", "up"):
        ticks[t0].append((here.has[name], functools.partial(start, "z", here.a, here.peer[name])))
        sends.append((here.has[name], "z", here.a))
    chain(t0, post, here.a, None)
    for s in range(1, here.slabs):
        for slab, come, to in (
            (here.a - s, here.a >= s, "up"),
            (here.a + s, here.a + s < here.slabs, "down"),
        ):
            both = jnp.logical_and(come, here.has[to])
            ticks[t0 + s].append((come, functools.partial(finish, "z", slab)))
            ticks[t0 + s].append((both, functools.partial(start, "z", slab, here.peer[to])))
            sends.append((both, "z", slab))
            chain(t0 + s, post, slab, come)

    def drain():
        for cond, stage, slab in sends:
            when(cond, copy(stage, slab, "own", here.peer["x"]).wait_send)

    return ticks, drain


def when(cond, action):
    if cond is None:
        action()
    else:
        pl.when(cond)(action)


def merge(schedules, lag):
    longest = max(lag * i + len(s) for i, s in enumerate(schedules))
    for t in range(longest):
        for i, s in enumerate(schedules):
            k = t - lag * i
            if 0 <= k < len(s):
                for cond, action in s[k]:
                    when(cond, action)


def parts_of(rows):
    return 4 if rows >= 64 else 1


def gather_kernel(slabs, layout, lag, *refs):
    count = len(layout["shapes"])
    shards, fulls = refs[:count], refs[count : 2 * count]
    send_sem, recv_sem, own_sem = refs[2 * count :]
    place = Place(slabs)
    local = []
    for i, (shard, full) in enumerate(zip(shards, fulls)):
        n = shard.shape[2]
        columns = pl.ds(pl.multiple_of(place.x * n, 128), n)
        own = pltpu.make_async_copy(
            shard, full.at[:, place.a, place.y, place.c, :, columns], own_sem.at[i]
        )
        own.start()
        local.append(own)
    place.greet()
    for own in local:
        own.wait()
    schedules, drains = [], []
    base = 0
    for i, plane0, planes in layout["groups"]:
        rows, n = shards[i].shape[1:]
        parts = parts_of(rows)
        size = rows // parts
        both = []
        for p in range(parts):
            ticks, drain = gather_ticks(
                place, fulls[i], pl.ds(plane0, planes), pl.ds(p * size, size), n,
                ORDERS[p], send_sem, recv_sem, base,
            )
            base += 1
            both.append(ticks)
            drains.append(drain)
        length = max(len(t) for t in both)
        schedules.append([sum((t[k] for t in both if k < len(t)), []) for k in range(length)])
    merge(schedules, lag)
    for drain in drains:
        drain()


def gather_all(shards, groups, dp, tensor, lag=2):
    slabs = dp // 4
    shapes = [s.shape for s in shards]
    parts = parts_of(shapes[0][1])
    bases = len(groups) * parts
    out = [
        jax.ShapeDtypeStruct((s[0], slabs, 2, 2, s[1], s[2] * tensor), jnp.bfloat16) for s in shapes
    ]
    full = pl.pallas_call(
        functools.partial(gather_kernel, slabs, {"shapes": shapes, "groups": groups}, lag),
        out_shape=out,
        in_specs=[pl.BlockSpec(memory_space=pltpu.VMEM)] * len(shards),
        out_specs=[pl.BlockSpec(memory_space=pl.ANY)] * len(shards),
        scratch_shapes=[
            pltpu.SemaphoreType.DMA((bases, 4, slabs)),
            pltpu.SemaphoreType.DMA((bases, 4, slabs)),
            pltpu.SemaphoreType.DMA((len(shards),)),
        ],
        compiler_params=pltpu.CompilerParams(collective_id=0, has_side_effects=True),
        name="gather_weights",
    )(*shards)
    return [f.reshape(s[0], dp * s[1], s[2] * tensor) for f, s in zip(full, shapes)]


def add_into(target, extra):
    lead = target.shape[:-2]
    count = 1
    for d in lead:
        count *= d
    for k in range(count):
        at = []
        for d in reversed(lead):
            at.insert(0, k % d)
            k = k // d
        target[tuple(at)] = target[tuple(at)] + extra[tuple(at)]


class PartSum:
    def __init__(self, place, src, out, planes, rows, n, order, bufs, sems, base):
        self.place, self.src, self.out = place, src, out
        self.planes, self.rows, self.n, self.order = planes, rows, n, order
        self.acc, self.got = bufs["acc"], bufs
        self.load_sem, self.send_sem, self.recv_sem = sems
        self.base = base
        self.sends = []

    def cut(self, ref, slab, y, x):
        place = self.place
        y = slice(None) if y == "all" else pl.ds(pick(place.y, y), 1)
        n = self.n
        x = slice(None) if x == "all" else pl.ds(pl.multiple_of(pick(place.x, x) * n, 128), n)
        return ref.at[:, slab, y, :, x]

    def span(self, stage, side):
        i = self.order.index(stage)
        sel = {d: ("all" if d in self.order[:i] else "own") for d in "xy"}
        if stage in "xy":
            sel[stage] = side
        return sel["y"], sel["x"]

    def load(self, slab):
        return pltpu.make_async_copy(
            self.src.at[self.planes, slab, :, self.place.c, self.rows, :],
            self.acc.at[:, slab],
            self.load_sem.at[self.base, slab],
        )

    def copy(self, stage, slab, peer, slot=None):
        k = STAGES[stage]
        slot = slab if slot is None else slot
        if stage == "c":
            ref = self.src.at[self.planes, slab, :, 1 - self.place.c, self.rows, :]
        else:
            ref = self.cut(self.acc, slab, *self.span(stage, "other"))
        into = self.got[stage]
        into = into.at[:, 0] if (stage != "c" and "z" in self.order[self.order.index(stage) :][1:]) else into.at[:, slot]
        return pltpu.make_async_remote_copy(
            ref, into, self.send_sem.at[self.base, k, slot], self.recv_sem.at[self.base, k, slot],
            peer, MESH,
        )

    def start(self, stage, slab):
        self.copy(stage, slab, self.place.peer[stage]).start()

    def begin(self, slab):
        self.load(slab).start()
        self.start("c", slab)

    def take(self, stage, slab, slot=None):
        copy = self.copy(stage, slab, self.place.peer["x"], slot)
        copy.wait_recv()
        slot = slab if slot is None else slot
        if stage == "c":
            self.load(slab).wait()
            add_into(self.acc.at[:, slab], self.got["c"].at[:, slot])
            return
        first = "z" in self.order[self.order.index(stage) :][1:]
        add_into(
            self.cut(self.acc, slab, *self.span(stage, "own")),
            self.got[stage].at[:, 0 if first else slot],
        )

    def take_z(self, slab, slot):
        self.take("z", slab, slot)

    def send_z(self, slab, to):
        place = self.place
        target = place.a + (1 if to == "up" else -1)
        slot = slab if to == "up" else jnp.where(slab == target, place.slabs, slab)
        self.copy("z", slab, place.peer[to], slot).start()

    def finish(self):
        place = self.place
        y, x = "own", "own"
        rows = self.rows
        self.out[:, rows, :] = self.cut(self.acc, place.a, y, x)[:, 0].astype(jnp.float32)

    def ticks(self):
        place, order = self.place, self.order
        zi = order.index("z")
        after = "c" + "".join(reversed(order[zi + 1 :]))
        before = "".join(reversed(order[:zi]))
        slabs = place.slabs
        ticks = [[] for _ in range(slabs + len(after) + len(before) + 2)]
        bind = functools.partial

        def early(t, slab, cond):
            ticks[t].append((cond, bind(self.begin, slab)))
            self.sends.append((cond, "c", slab, None))
            for i, stage in enumerate(after):
                ticks[t + i + 1].append((cond, bind(self.take, stage, slab)))
                if i + 1 < len(after):
                    ticks[t + i + 1].append((cond, bind(self.start, after[i + 1], slab)))
                    self.sends.append((cond, after[i + 1], slab, None))

        z0 = len(after)
        for k, s in enumerate(range(slabs - 1, 0, -1)):
            for slab, cond, to, more in (
                (place.a + s, place.a + s < slabs, "up", place.has["down"]),
                (place.a - s, place.a >= s, "down", place.has["up"]),
            ):
                early(k, slab, cond)
                both = jnp.logical_and(cond, more)
                ticks[z0 + k].append((both, bind(self.take_z, slab, slab)))
                ticks[z0 + k].append((cond, bind(self.send_z, slab, to)))
                self.sends.append((cond, "z", slab, to))
        last = slabs - 1
        early(last, place.a, None)
        ticks[z0 + last].append((place.has["down"], bind(self.take_z, place.a, place.a)))
        ticks[z0 + last].append((place.has["up"], bind(self.take_z, place.a, slabs)))
        t = z0 + last
        for stage in before:
            ticks[t].append((None, bind(self.start, stage, place.a)))
            self.sends.append((None, stage, place.a, None))
            ticks[t + 1].append((None, bind(self.take, stage, place.a)))
            t += 1
        ticks[t].append((None, self.finish))
        return ticks

    def drain(self):
        place = self.place
        for cond, stage, slab, to in self.sends:
            slot = None
            if to == "down":
                slot = jnp.where(slab == place.a - 1, place.slabs, slab)
            when(cond, self.copy(stage, slab, place.peer["x"], slot).wait_send)


def sum_buffers(planes, slabs, size, n, tensor, order):
    cols = n * tensor
    shapes = {"acc": (planes, slabs, 2, size, cols), "c": (planes, slabs, 2, size, cols)}
    for i, d in enumerate(order):
        ys = 2 if "y" in order[:i] else 1
        xs = cols if "x" in order[:i] else n
        count = slabs + 1 if d == "z" else (1 if "z" in order[i + 1 :] else slabs)
        shapes[d] = (planes, count, ys, size, xs)
    return shapes


def small_sum(place, mine, total, got, sems):
    send_sem, recv_sem = sems
    steps = []

    def exchange(k, name):
        return pltpu.make_async_remote_copy(
            total, got.at[k], send_sem.at[k], recv_sem.at[k], place.peer[name], MESH
        )

    def open_(k, name):
        exchange(k, name).start()

    def close(k, name):
        copy = exchange(k, name)
        copy.wait_send()
        copy.wait_recv()
        total[...] = total[...] + got[k]

    def begin():
        total[...] = mine[...]

    def chain(slab):
        return pltpu.make_async_remote_copy(
            total, got.at[3 + place.a], send_sem.at[3 + slab], recv_sem.at[3 + place.a],
            (place.dp + 4 * (slab - place.a), place.x), MESH,
        )

    def arrival(slab):
        return pltpu.make_async_remote_copy(
            total, got.at[3 + slab], send_sem.at[3 + slab], recv_sem.at[3 + slab],
            (place.dp, place.x), MESH,
        )

    def spread():
        for slab in range(place.slabs):
            pl.when(slab != place.a)(lambda slab=slab: chain(slab).start())

    def collect():
        for slab in range(place.slabs):

            def wait(slab=slab):
                chain(slab).wait_send()
                arrival(slab).wait_recv()

            pl.when(slab != place.a)(wait)
        got[3 + place.a] = total[...]
        value = got[3]
        for slab in range(1, place.slabs):
            value = value + got[3 + slab]
        total[...] = value

    names = "cxy"
    steps.append([begin, functools.partial(open_, 0, "c")])
    for k, name in enumerate(names):
        then = functools.partial(open_, k + 1, names[k + 1]) if k < 2 else spread
        steps.append([functools.partial(close, k, name), then])
    steps.append([collect])
    return [[(None, action) for action in step] for step in steps]


def sum_kernel(slabs, tensor, groups, lag, count, *refs):
    parts_in, small = refs[:count], refs[count]
    outs, small_out = refs[count + 1 : 2 * count + 1], refs[2 * count + 1]
    scratch = list(refs[2 * count + 2 :])
    load_sem, send_sem, recv_sem, small_got, small_send, small_recv = scratch[:6]
    scratch = scratch[6:]
    place = Place(slabs)
    place.greet(chain=True)
    schedules, jobs, base = [], [], 0
    for i, plane0, planes in groups:
        rows, n = outs[i].shape[1:]
        parts = parts_of(rows)
        size = rows // parts
        both = []
        for p in range(parts):
            names = sum_buffers(planes, slabs, size, n, tensor, ORDERS[p])
            bufs = {name: scratch.pop(0) for name in names}
            job = PartSum(
                place, parts_in[i], outs[i].at[pl.ds(plane0, planes)],
                pl.ds(plane0, planes), pl.ds(p * size, size), n, ORDERS[p], bufs,
                (load_sem, send_sem, recv_sem), base,
            )
            base += 1
            both.append(job.ticks())
            jobs.append(job)
        length = max(len(t) for t in both)
        schedules.append([sum((t[k] for t in both if k < len(t)), []) for k in range(length)])
    schedules.append(small_sum(place, small, small_out, small_got, (small_send, small_recv)))
    merge(schedules, lag)
    for job in jobs:
        job.drain()


def sum_all(partials, small, groups, dp, tensor, lag=2):
    slabs = dp // 4
    wide, outs = [], []
    for part in partials:
        planes, rows, cols = part.shape
        wide.append(part.reshape(planes, slabs, 2, 2, rows // dp, cols))
        outs.append(jax.ShapeDtypeStruct((planes, rows // dp, cols // tensor), jnp.float32))
    scratch, bases = [], 0
    for i, _, planes in groups:
        rows, n = outs[i].shape[1:]
        parts = parts_of(rows)
        for p in range(parts):
            shapes = sum_buffers(planes, slabs, rows // parts, n, tensor, ORDERS[p])
            scratch += [pltpu.VMEM(shape, jnp.bfloat16) for shape in shapes.values()]
            bases += 1
    dma = pltpu.SemaphoreType.DMA
    vmem = pl.BlockSpec(memory_space=pltpu.VMEM)
    return pl.pallas_call(
        functools.partial(sum_kernel, slabs, tensor, groups, lag, len(partials)),
        out_shape=[*outs, jax.ShapeDtypeStruct(small.shape, jnp.float32)],
        in_specs=[pl.BlockSpec(memory_space=pl.ANY)] * len(partials) + [vmem],
        out_specs=[vmem] * (len(partials) + 1),
        scratch_shapes=[
            dma((bases, slabs)),
            dma((bases, 4, slabs + 1)),
            dma((bases, 4, slabs + 1)),
            pltpu.VMEM((3 + slabs, *small.shape), jnp.float32),
            dma((3 + slabs,)),
            dma((3 + slabs,)),
            *scratch,
        ],
        compiler_params=pltpu.CompilerParams(
            collective_id=1, has_side_effects=True, vmem_limit_bytes=67043328
        ),
        name="sum_gradients",
    )(*wide, small)


TILE = 512
AHEAD = 3


def far_first(place):
    slabs = place.slabs
    tables = []
    for a in range(slabs):
        tables.append(sorted(range(slabs), key=lambda k: (-abs(k - a), -k)))
    return [
        sum(jnp.where(place.a == a, tables[a][i], 0) for a in range(slabs)) for i in range(slabs)
    ]


class TilePart(PartSum):
    def ticks(self, order_of_slabs):
        place, order = self.place, self.order
        zi = order.index("z")
        after = "".join(reversed(order[zi + 1 :]))
        before = "".join(reversed(order[:zi]))
        slabs = place.slabs
        ticks = {}
        bind = functools.partial

        def put(t, unit, cond, action):
            ticks.setdefault(t, []).append((unit, cond, action))

        def begin(stage, slab):
            self.sends.append((None, stage, slab, None))
            return bind(self.start, stage, slab)

        for i, slab in enumerate(order_of_slabs):
            t = i + 1
            for stage in after:
                put(t, i, None, begin(stage, slab))
                put(t + 1, i, None, bind(self.take, stage, slab))
                t += 1
            if i < slabs - 1:
                up, down = slab > place.a, slab < place.a
                from_both = jnp.logical_or(
                    jnp.logical_and(up, place.has["down"]), jnp.logical_and(down, place.has["up"])
                )
                put(t, i, from_both, bind(self.take_z, slab, slab))
                for cond, to in ((up, "up"), (down, "down")):
                    put(t, i, cond, bind(self.send_z, slab, to))
                    self.sends.append((cond, "z", slab, to))
                continue
            put(t, i, place.has["down"], bind(self.take_z, slab, slab))
            put(t, i, place.has["up"], bind(self.take_z, slab, slabs))
            for stage in before:
                put(t, i, None, begin(stage, slab))
                put(t + 1, i, None, bind(self.take, stage, slab))
                t += 1
            put(t, i, None, self.finish)
        return ticks


def tile_sum_kernel(slabs, tensor, groups, a_count, b_count, out_count, *refs):
    lefts, refs = refs[:a_count], refs[a_count:]
    rights, refs = refs[:b_count], refs[b_count:]
    small, refs = refs[0], refs[1:]
    outs, small_out, refs = refs[:out_count], refs[out_count], refs[out_count + 1 :]
    send_sem, recv_sem, core_send, core_recv, small_got, small_send, small_recv = refs[:7]
    left_buf, left_sem, turned, right_buf, right_sem = refs[7:12]
    scratch = list(refs[12:])
    place = Place(slabs)
    place.greet(chain=True)
    sigma = far_first(place)
    units = [(g, i) for g in range(len(groups)) for i in range(slabs)]
    block = 4 * outs[0].shape[1]

    def left_copy(u):
        g, i = units[u]
        at = pl.ds(pl.multiple_of(sigma[i] * block, 128), block)
        return pltpu.make_async_copy(
            lefts[groups[g][0]].at[:, at], left_buf.at[u % 2], left_sem.at[u % 2]
        )

    def right_copy(g, k):
        right = rights[groups[g][1]]
        wide = right.shape[2] // TILE
        at = pl.ds(pl.multiple_of((k % wide) * TILE, TILE), TILE)
        slot = k % (AHEAD + 1)
        return pltpu.make_async_copy(
            right.at[k // wide, :, at], right_buf.at[slot], right_sem.at[slot]
        )

    def multiply(u, tile):
        g = units[u][0]
        right = rights[groups[g][1]]
        wide = right.shape[2] // TILE
        steps = right.shape[0] * wide
        left_copy(u).wait()
        if u + 1 < len(units):
            left_copy(u + 1).start()
        turned[...] = left_buf[u % 2].T

        def body(k, carry):
            right_copy(g, k).wait()

            @pl.when(k + AHEAD < steps)
            def _():
                right_copy(g, k + AHEAD).start()

            product = jnp.dot(
                turned[...], right_buf[k % (AHEAD + 1)], preferred_element_type=jnp.float32
            )
            at = pl.ds(pl.multiple_of((k % wide) * TILE, TILE), TILE)
            tile[k // wide, :, :, :, at] = product.reshape(2, 2, block // 4, TILE).astype(
                tile.dtype
            )
            return carry

        lax.fori_loop(0, steps, body, 0)
        if u + 1 < len(units):
            preload(u + 1)

    def preload(u):
        g = units[u][0]
        right = rights[groups[g][1]]
        for k in range(min(AHEAD, right.shape[0] * (right.shape[2] // TILE))):
            right_copy(g, k).start()

    schedule, jobs, base = {}, [], 0
    tiles = {}

    def put(t, rank, cond, action):
        schedule.setdefault(t, []).append((rank, cond, action))

    for g, (_, ri, oi, plane0) in enumerate(groups):
        rows, n = outs[oi].shape[1:]
        planes = rights[ri].shape[0]
        key = (planes, n)
        if key not in tiles:
            tiles[key] = scratch.pop(0)
        acc = scratch.pop(0)
        tile_pair = tiles[key]
        parts = parts_of(rows)
        size = rows // parts

        def core_copy(u, g=g, acc=acc, tile_pair=tile_pair):
            slab = sigma[units[u][1]]
            return pltpu.make_async_remote_copy(
                tile_pair.at[u % 2, :, :, 1 - place.c],
                acc.at[:, slab],
                core_send.at[g, slab],
                core_recv.at[g, slab],
                place.peer["c"],
                MESH,
            )

        def make(u, tile_pair=tile_pair, core_copy=core_copy):
            multiply(u, tile_pair.at[u % 2])
            core_copy(u).start()

        def join(u, acc=acc, tile_pair=tile_pair, core_copy=core_copy):
            copy = core_copy(u)
            copy.wait_send()
            copy.wait_recv()
            add_into(
                acc.at[:, sigma[units[u][1]]], tile_pair.at[u % 2, :, :, place.c]
            )

        for i in range(slabs):
            u = g * slabs + i
            put(u, (1, 0), None, functools.partial(make, u))
            put(u + 1, (0, 0), None, functools.partial(join, u))
        for p in range(parts):
            shapes = sum_buffers(planes, slabs, size, n, tensor, ORDERS[p])
            bufs = {name: scratch.pop(0) for name in "xyz"}
            bufs["acc"] = acc.at[:, :, :, pl.ds(p * size, size)]
            job = TilePart(
                place, None, outs[oi].at[pl.ds(plane0, planes)], None, pl.ds(p * size, size), n,
                ORDERS[p], bufs, (None, send_sem, recv_sem), base,
            )
            base += 1
            jobs.append(job)
            for t, actions in job.ticks(sigma).items():
                for k, (i, cond, action) in enumerate(actions):
                    u = g * slabs + i
                    first = t == i + 1 and getattr(action, "func", None) == job.start
                    rank = (0, 1 + p) if first else (2, -u)
                    put(g * slabs + t, rank, cond, action)
    for t, actions in enumerate(small_sum(place, small, small_out, small_got, (small_send, small_recv))):
        for cond, action in actions:
            put(t + 1, (3, 0), cond, action)
    left_copy(0).start()
    preload(0)
    for t in sorted(schedule):
        for _, cond, action in sorted(schedule[t], key=lambda item: item[0]):
            when(cond, action)
    for job in jobs:
        job.drain()


def tile_sum_all(lefts, rights, outs, groups, small, dp, tensor):
    slabs = dp // 4
    bf = jnp.bfloat16
    seen, scratch, bases = set(), [], 0
    for _, ri, oi, _ in groups:
        planes = rights[ri].shape[0]
        rows, n = outs[oi].shape[1:]
        cols = n * tensor
        if (planes, n) not in seen:
            seen.add((planes, n))
            scratch.append(pltpu.VMEM((2, planes, 2, 2, rows, cols), bf))
        scratch.append(pltpu.VMEM((planes, slabs, 2, rows, cols), bf))
        parts = parts_of(rows)
        for p in range(parts):
            shapes = sum_buffers(planes, slabs, rows // parts, n, tensor, ORDERS[p])
            scratch += [pltpu.VMEM(shapes[name], bf) for name in "xyz"]
            bases += 1
    dma = pltpu.SemaphoreType.DMA
    vmem = pl.BlockSpec(memory_space=pltpu.VMEM)
    depth = lefts[0].shape[0]
    block = 4 * outs[0].shape[1]
    return pl.pallas_call(
        functools.partial(
            tile_sum_kernel, slabs, tensor, groups, len(lefts), len(rights), len(outs)
        ),
        out_shape=[*outs, jax.ShapeDtypeStruct(small.shape, jnp.float32)],
        in_specs=[pl.BlockSpec(memory_space=pl.ANY)] * (len(lefts) + len(rights)) + [vmem],
        out_specs=[vmem] * (len(outs) + 1),
        scratch_shapes=[
            dma((bases, 4, slabs + 1)),
            dma((bases, 4, slabs + 1)),
            dma((len(groups), slabs)),
            dma((len(groups), slabs)),
            pltpu.VMEM((3 + slabs, *small.shape), jnp.float32),
            dma((3 + slabs,)),
            dma((3 + slabs,)),
            pltpu.VMEM((2, depth, block), bf),
            dma((2,)),
            pltpu.VMEM((block, depth), bf),
            pltpu.VMEM((AHEAD + 1, depth, TILE), bf),
            dma((AHEAD + 1,)),
            *scratch,
        ],
        compiler_params=pltpu.CompilerParams(
            collective_id=2, has_side_effects=True, vmem_limit_bytes=67043328
        ),
        name="sum_products",
    )(*lefts, *rights, small)


def per_device(
    tokens,
    gain_mix,
    in_weight,
    conv_weight,
    out_weight,
    gain_ff,
    gate_up_weight,
    down_weight,
    grad_out,
):
    inputs = tokens.astype(jnp.float32)
    dp, tensor = lax.axis_size("dp"), lax.axis_size("tensor")
    in_full, out_full, gate_up_full, down_full = gather_all(
        [in_weight, out_weight[None], gate_up_weight, down_weight[None]], GROUPS, dp, tensor
    )
    out_full, down_full = out_full[0], down_full[0]
    rows, width = tokens.shape
    seq_count = rows // LEN
    scale_mix = norm_scale(inputs)
    normed_mix = (inputs * scale_mix * gain_mix).astype(jnp.bfloat16)
    projected = jnp.einsum("gd,jdc->jgc", normed_mix, in_full, preferred_element_type=jnp.float32)
    shaped = (seq_count, LEN, width)
    input_gate = projected[0].reshape(shaped)
    output_gate = projected[1].reshape(shaped)
    value_part = projected[2].reshape(shaped)
    mixed_in = input_gate * value_part
    conv_out = (
        conv_weight[0] * delayed(mixed_in, 2)
        + conv_weight[1] * delayed(mixed_in, 1)
        + conv_weight[2] * mixed_in
    )
    gated_rows = (output_gate * conv_out).astype(jnp.bfloat16).reshape(rows, width)
    residual = inputs + lax.dot_general(
        gated_rows, out_full, (((1,), (1,)), ((), ())), preferred_element_type=jnp.float32
    )
    scale_ff = norm_scale(residual)
    normed_ff = (residual * scale_ff * gain_ff).astype(jnp.bfloat16)
    gate_up = jnp.einsum(
        "gd,jdf->jgf", normed_ff, gate_up_full, preferred_element_type=jnp.float32
    )
    gate_pre = gate_up[0]
    up_value = gate_up[1]
    sigmoid_gate = jax.nn.sigmoid(gate_pre)
    silu_gate = gate_pre * sigmoid_gate
    hidden = (silu_gate * up_value).astype(jnp.bfloat16)
    block_out = (
        residual
        + lax.dot_general(
            hidden, down_full, (((1,), (1,)), ((), ())), preferred_element_type=jnp.float32
        )
    ).astype(jnp.bfloat16)
    hidden_grad = jnp.dot(grad_out, down_full, preferred_element_type=jnp.float32)
    silu_slope = sigmoid_gate * (1.0 + gate_pre * (1.0 - sigmoid_gate))
    gate_grad = (hidden_grad * up_value * silu_slope).astype(jnp.bfloat16)
    up_grad = (hidden_grad * silu_gate).astype(jnp.bfloat16)
    gate_up_grad = jnp.stack([gate_grad, up_grad])
    ffn_in_grad = jnp.einsum(
        "jgf,jdf->gd", gate_up_grad, gate_up_full, preferred_element_type=jnp.float32
    )
    residual_back, gain_ff_grad = norm_back(residual, scale_ff, gain_ff, ffn_in_grad)
    residual_grad = grad_out.astype(jnp.float32) + residual_back
    mixer_grads = residual_grad.astype(jnp.bfloat16)
    gated_grad = jnp.dot(mixer_grads, out_full, preferred_element_type=jnp.float32).reshape(shaped)
    output_gate_grad = gated_grad * conv_out
    conv_grad_in = gated_grad * output_gate
    mixed_grad = (
        conv_weight[2] * conv_grad_in
        + conv_weight[1] * advanced(conv_grad_in, 1)
        + conv_weight[0] * advanced(conv_grad_in, 2)
    )
    tap_grads = jnp.stack(
        [
            jnp.sum(conv_grad_in * delayed(mixed_in, 2), axis=(0, 1)),
            jnp.sum(conv_grad_in * delayed(mixed_in, 1), axis=(0, 1)),
            jnp.sum(conv_grad_in * mixed_in, axis=(0, 1)),
        ]
    )
    proj_grad = (
        jnp.stack([mixed_grad * value_part, output_gate_grad, mixed_grad * input_gate])
        .astype(jnp.bfloat16)
        .reshape(3, rows, width)
    )
    mixer_in_grad = jnp.einsum(
        "jgc,jdc->gd", proj_grad, in_full, preferred_element_type=jnp.float32
    )
    input_back, gain_mix_grad = norm_back(inputs, scale_mix, gain_mix, mixer_in_grad)
    input_grad = residual_grad + input_back
    small = jnp.concatenate(
        [gain_mix_grad[None], gain_ff_grad[None], tap_grads, jnp.zeros((3, width), jnp.float32)]
    )
    if in_weight.shape[1] >= 64:
        shards = (down_weight[None], gate_up_weight, in_weight, out_weight[None])
        down_sum, gate_up_sum, in_sum, out_sum, small_sums = tile_sum_all(
            [grad_out, normed_ff, normed_mix, mixer_grads],
            [hidden[None], gate_grad[None], up_grad[None], proj_grad, gated_rows[None]],
            [jax.ShapeDtypeStruct(shard.shape, jnp.float32) for shard in shards],
            PRODUCTS,
            small,
            dp,
            tensor,
        )
    else:
        down_grad = lax.dot_general(
            grad_out, hidden, (((0,), (0,)), ((), ())), preferred_element_type=jnp.float32
        )
        gate_up_weight_grad = jnp.einsum(
            "gd,jgf->jdf", normed_ff, gate_up_grad, preferred_element_type=jnp.float32
        )
        out_weight_grad = lax.dot_general(
            mixer_grads, gated_rows, (((0,), (0,)), ((), ())), preferred_element_type=jnp.float32
        )
        in_weight_grad = jnp.einsum(
            "gd,jgc->jdc", normed_mix, proj_grad, preferred_element_type=jnp.float32
        )
        down_sum, gate_up_sum, in_sum, out_sum, small_sums = sum_all(
            [
                down_grad.astype(jnp.bfloat16)[None],
                gate_up_weight_grad.astype(jnp.bfloat16),
                in_weight_grad.astype(jnp.bfloat16),
                out_weight_grad.astype(jnp.bfloat16)[None],
            ],
            small,
            SUM_GROUPS,
            dp,
            tensor,
        )
    return (
        block_out,
        input_grad,
        small_sums[0],
        in_sum,
        small_sums[2:5],
        out_sum[0],
        small_sums[1],
        gate_up_sum,
        down_sum[0],
    )


def solution(mesh):
    in_specs = (
        P(("dp", "tensor"), None),
        P(),
        P(None, "dp", "tensor"),
        P(),
        P("dp", "tensor"),
        P(),
        P(None, "dp", "tensor"),
        P("dp", "tensor"),
        P(("dp", "tensor"), None),
    )
    out_specs = (
        P(("dp", "tensor"), None),
        P(("dp", "tensor"), None),
        P(),
        P(None, "dp", "tensor"),
        P(),
        P("dp", "tensor"),
        P(),
        P(None, "dp", "tensor"),
        P("dp", "tensor"),
    )
    return jax.shard_map(
        per_device, mesh=mesh, in_specs=in_specs, out_specs=out_specs, check_vma=False
    )
```

```python
import functools

import jax
import jax.numpy as jnp
from jax import lax
from jax.experimental import pallas as pl
from jax.experimental.pallas import tpu as pltpu
from jax.sharding import PartitionSpec as P

LEN = 1024


EPS = 1e-05


def norm_scale(values):
    return lax.rsqrt(jnp.mean(values * values, axis=-1, keepdims=True) + EPS)


def delayed(values, shift_by):
    return jnp.pad(values[:, : values.shape[1] - shift_by], ((0, 0), (shift_by, 0), (0, 0)))


def advanced(values, shift_by):
    return jnp.pad(values[:, shift_by:], ((0, 0), (0, shift_by), (0, 0)))


def norm_back(values, row_scale, gain_vec, grad_normed):
    weighted = grad_normed * gain_vec
    inner_mean = jnp.mean(weighted * values, axis=-1, keepdims=True)
    grad_values = row_scale * weighted - values * row_scale**3 * inner_mean
    gain_grad = jnp.sum(grad_normed * values * row_scale, axis=0)
    return (grad_values, gain_grad)


MESH = pl.DeviceIdType.MESH
ORDERS = ("xzy", "yzx", "zxy", "zyx")
GROUPS = ((0, 0, 3), (1, 0, 1), (2, 0, 1), (2, 1, 1), (3, 0, 1))
SUM_GROUPS = ((0, 0, 1), (1, 0, 1), (1, 1, 1), (2, 0, 3), (3, 0, 1))
PRODUCTS = ((0, 0, 0, 0), (1, 1, 1, 0), (1, 2, 1, 1), (2, 3, 2, 0), (3, 4, 3, 0))
STARTS = (0, 1, 3, 5, 7)
STAGES = {"x": 0, "y": 1, "z": 2, "c": 3}


class Place:
    def __init__(self, slabs):
        dp = lax.axis_index("dp")
        self.dp, self.x = dp, lax.axis_index("tensor")
        self.slabs = slabs
        self.a = dp // 4
        self.y = (dp // 2) % 2
        self.c = dp % 2
        self.peer = {
            "x": (dp, 1 - self.x),
            "y": (dp + 2 - 4 * self.y, self.x),
            "c": (dp + 1 - 2 * self.c, self.x),
            "down": (dp - 4, self.x),
            "up": (dp + 4, self.x),
        }
        self.has = {"down": self.a > 0, "up": self.a < slabs - 1}

    def greet(self, chain=False):
        barrier = pltpu.get_barrier_semaphore()
        for name in ("x", "y", "c"):
            pl.semaphore_signal(barrier, 1, device_id=self.peer[name], device_id_type=MESH)
        if chain:
            for slab in range(self.slabs):

                @pl.when(slab != self.a)
                def _(slab=slab):
                    pl.semaphore_signal(
                        barrier,
                        1,
                        device_id=(self.dp + 4 * (slab - self.a), self.x),
                        device_id_type=MESH,
                    )

            pl.semaphore_wait(barrier, 2 + self.slabs)
            return
        for name in ("down", "up"):

            @pl.when(self.has[name])
            def _(name=name):
                pl.semaphore_signal(barrier, 1, device_id=self.peer[name], device_id_type=MESH)

        ends = self.has["down"].astype(jnp.int32) + self.has["up"].astype(jnp.int32)
        pl.semaphore_wait(barrier, 3 + ends)


def pick(own, which):
    if which == "all":
        return slice(None)
    return own if which == "own" else 1 - own


def gather_ticks(place, full, planes, rows, cols, order, send_sem, recv_sem, base):
    here = place
    n = cols

    def region(slab, y, c, x):
        columns = slice(None) if x == "all" else pl.ds(pl.multiple_of(pick(here.x, x) * n, 128), n)
        return full.at[planes, slab, pick(here.y, y), pick(here.c, c), rows, columns]

    def span(stage, side):
        i = order.index(stage) if stage != "c" else 3
        done = order[:i]
        sel = {d: ("all" if d in done else "own") for d in "xy"}
        if stage in "xy":
            sel[stage] = side
        return sel["y"], (side if stage == "c" else "own"), sel["x"]

    def copy(stage, slab, side, peer):
        ref = region(slab, *span(stage, side))
        k = STAGES[stage]
        return pltpu.make_async_remote_copy(
            ref, ref, send_sem.at[base, k, slab], recv_sem.at[base, k, slab], peer, MESH
        )

    zi = order.index("z")
    pre, post = order[:zi], order[zi + 1 :] + "c"
    total = len(pre) + here.slabs + len(post) + 1
    ticks = [[] for _ in range(total)]
    sends = []

    def start(stage, slab, peer):
        copy(stage, slab, "own", peer).start()

    def finish(stage, slab):
        copy(stage, slab, "own" if stage == "z" else "other", here.peer["x"]).wait_recv()

    def chain(t, stages, slab, cond):
        for i, stage in enumerate(stages):
            ticks[t + i].append((cond, functools.partial(start, stage, slab, here.peer[stage])))
            ticks[t + i + 1].append((cond, functools.partial(finish, stage, slab)))
            sends.append((cond, stage, slab))

    chain(0, pre, here.a, None)
    t0 = len(pre)
    for name in ("down", "up"):
        ticks[t0].append((here.has[name], functools.partial(start, "z", here.a, here.peer[name])))
        sends.append((here.has[name], "z", here.a))
    chain(t0, post, here.a, None)
    for s in range(1, here.slabs):
        for slab, come, to in (
            (here.a - s, here.a >= s, "up"),
            (here.a + s, here.a + s < here.slabs, "down"),
        ):
            both = jnp.logical_and(come, here.has[to])
            ticks[t0 + s].append((come, functools.partial(finish, "z", slab)))
            ticks[t0 + s].append((both, functools.partial(start, "z", slab, here.peer[to])))
            sends.append((both, "z", slab))
            chain(t0 + s, post, slab, come)

    def drain():
        for cond, stage, slab in sends:
            when(cond, copy(stage, slab, "own", here.peer["x"]).wait_send)

    return ticks, drain


def when(cond, action):
    if cond is None:
        action()
    else:
        pl.when(cond)(action)


def merge(schedules, lag):
    longest = max(lag * i + len(s) for i, s in enumerate(schedules))
    for t in range(longest):
        for i, s in enumerate(schedules):
            k = t - lag * i
            if 0 <= k < len(s):
                for cond, action in s[k]:
                    when(cond, action)


def parts_of(rows):
    return 4 if rows >= 64 else 1


def add_into(target, extra):
    lead = target.shape[:-2]
    count = 1
    for d in lead:
        count *= d
    for k in range(count):
        at = []
        for d in reversed(lead):
            at.insert(0, k % d)
            k = k // d
        target[tuple(at)] = target[tuple(at)] + extra[tuple(at)]


class PartSum:
    def __init__(self, place, src, out, planes, rows, n, order, bufs, sems, base):
        self.place, self.src, self.out = place, src, out
        self.planes, self.rows, self.n, self.order = planes, rows, n, order
        self.acc, self.got = bufs["acc"], bufs
        self.load_sem, self.send_sem, self.recv_sem = sems
        self.base = base
        self.sends = []

    def cut(self, ref, slab, y, x):
        place = self.place
        y = slice(None) if y == "all" else pl.ds(pick(place.y, y), 1)
        n = self.n
        x = slice(None) if x == "all" else pl.ds(pl.multiple_of(pick(place.x, x) * n, 128), n)
        return ref.at[:, slab, y, :, x]

    def span(self, stage, side):
        i = self.order.index(stage)
        sel = {d: ("all" if d in self.order[:i] else "own") for d in "xy"}
        if stage in "xy":
            sel[stage] = side
        return sel["y"], sel["x"]

    def load(self, slab):
        return pltpu.make_async_copy(
            self.src.at[self.planes, slab, :, self.place.c, self.rows, :],
            self.acc.at[:, slab],
            self.load_sem.at[self.base, slab],
        )

    def copy(self, stage, slab, peer, slot=None):
        k = STAGES[stage]
        slot = slab if slot is None else slot
        if stage == "c":
            ref = self.src.at[self.planes, slab, :, 1 - self.place.c, self.rows, :]
        else:
            ref = self.cut(self.acc, slab, *self.span(stage, "other"))
        into = self.got[stage]
        into = into.at[:, 0] if (stage != "c" and "z" in self.order[self.order.index(stage) :][1:]) else into.at[:, slot]
        return pltpu.make_async_remote_copy(
            ref, into, self.send_sem.at[self.base, k, slot], self.recv_sem.at[self.base, k, slot],
            peer, MESH,
        )

    def start(self, stage, slab):
        self.copy(stage, slab, self.place.peer[stage]).start()

    def begin(self, slab):
        self.load(slab).start()
        self.start("c", slab)

    def take(self, stage, slab, slot=None):
        copy = self.copy(stage, slab, self.place.peer["x"], slot)
        copy.wait_recv()
        slot = slab if slot is None else slot
        if stage == "c":
            self.load(slab).wait()
            add_into(self.acc.at[:, slab], self.got["c"].at[:, slot])
            return
        first = "z" in self.order[self.order.index(stage) :][1:]
        add_into(
            self.cut(self.acc, slab, *self.span(stage, "own")),
            self.got[stage].at[:, 0 if first else slot],
        )

    def take_z(self, slab, slot):
        self.take("z", slab, slot)

    def send_z(self, slab, to):
        place = self.place
        target = place.a + (1 if to == "up" else -1)
        slot = slab if to == "up" else jnp.where(slab == target, place.slabs, slab)
        self.copy("z", slab, place.peer[to], slot).start()

    def finish(self):
        place = self.place
        y, x = "own", "own"
        rows = self.rows
        self.out[:, rows, :] = self.cut(self.acc, place.a, y, x)[:, 0].astype(jnp.float32)

    def ticks(self):
        place, order = self.place, self.order
        zi = order.index("z")
        after = "c" + "".join(reversed(order[zi + 1 :]))
        before = "".join(reversed(order[:zi]))
        slabs = place.slabs
        ticks = [[] for _ in range(slabs + len(after) + len(before) + 2)]
        bind = functools.partial

        def early(t, slab, cond):
            ticks[t].append((cond, bind(self.begin, slab)))
            self.sends.append((cond, "c", slab, None))
            for i, stage in enumerate(after):
                ticks[t + i + 1].append((cond, bind(self.take, stage, slab)))
                if i + 1 < len(after):
                    ticks[t + i + 1].append((cond, bind(self.start, after[i + 1], slab)))
                    self.sends.append((cond, after[i + 1], slab, None))

        z0 = len(after)
        for k, s in enumerate(range(slabs - 1, 0, -1)):
            for slab, cond, to, more in (
                (place.a + s, place.a + s < slabs, "up", place.has["down"]),
                (place.a - s, place.a >= s, "down", place.has["up"]),
            ):
                early(k, slab, cond)
                both = jnp.logical_and(cond, more)
                ticks[z0 + k].append((both, bind(self.take_z, slab, slab)))
                ticks[z0 + k].append((cond, bind(self.send_z, slab, to)))
                self.sends.append((cond, "z", slab, to))
        last = slabs - 1
        early(last, place.a, None)
        ticks[z0 + last].append((place.has["down"], bind(self.take_z, place.a, place.a)))
        ticks[z0 + last].append((place.has["up"], bind(self.take_z, place.a, slabs)))
        t = z0 + last
        for stage in before:
            ticks[t].append((None, bind(self.start, stage, place.a)))
            self.sends.append((None, stage, place.a, None))
            ticks[t + 1].append((None, bind(self.take, stage, place.a)))
            t += 1
        ticks[t].append((None, self.finish))
        return ticks

    def drain(self):
        place = self.place
        for cond, stage, slab, to in self.sends:
            slot = None
            if to == "down":
                slot = jnp.where(slab == place.a - 1, place.slabs, slab)
            when(cond, self.copy(stage, slab, place.peer["x"], slot).wait_send)


def sum_buffers(planes, slabs, size, n, tensor, order):
    cols = n * tensor
    shapes = {"acc": (planes, slabs, 2, size, cols), "c": (planes, slabs, 2, size, cols)}
    for i, d in enumerate(order):
        ys = 2 if "y" in order[:i] else 1
        xs = cols if "x" in order[:i] else n
        count = slabs + 1 if d == "z" else (1 if "z" in order[i + 1 :] else slabs)
        shapes[d] = (planes, count, ys, size, xs)
    return shapes


def small_sum(place, mine, total, got, sems):
    send_sem, recv_sem = sems
    steps = []

    def exchange(k, name):
        return pltpu.make_async_remote_copy(
            total, got.at[k], send_sem.at[k], recv_sem.at[k], place.peer[name], MESH
        )

    def open_(k, name):
        exchange(k, name).start()

    def close(k, name):
        copy = exchange(k, name)
        copy.wait_send()
        copy.wait_recv()
        total[...] = total[...] + got[k]

    def begin():
        total[...] = mine[...]

    def chain(slab):
        return pltpu.make_async_remote_copy(
            total, got.at[3 + place.a], send_sem.at[3 + slab], recv_sem.at[3 + place.a],
            (place.dp + 4 * (slab - place.a), place.x), MESH,
        )

    def arrival(slab):
        return pltpu.make_async_remote_copy(
            total, got.at[3 + slab], send_sem.at[3 + slab], recv_sem.at[3 + slab],
            (place.dp, place.x), MESH,
        )

    def spread():
        for slab in range(place.slabs):
            pl.when(slab != place.a)(lambda slab=slab: chain(slab).start())

    def collect():
        for slab in range(place.slabs):

            def wait(slab=slab):
                chain(slab).wait_send()
                arrival(slab).wait_recv()

            pl.when(slab != place.a)(wait)
        got[3 + place.a] = total[...]
        value = got[3]
        for slab in range(1, place.slabs):
            value = value + got[3 + slab]
        total[...] = value

    names = "cxy"
    steps.append([begin, functools.partial(open_, 0, "c")])
    for k, name in enumerate(names):
        then = functools.partial(open_, k + 1, names[k + 1]) if k < 2 else spread
        steps.append([functools.partial(close, k, name), then])
    steps.append([collect])
    return [[(None, action) for action in step] for step in steps]


def sum_kernel(slabs, tensor, groups, lag, count, *refs):
    parts_in, small = refs[:count], refs[count]
    outs, small_out = refs[count + 1 : 2 * count + 1], refs[2 * count + 1]
    scratch = list(refs[2 * count + 2 :])
    load_sem, send_sem, recv_sem, small_got, small_send, small_recv = scratch[:6]
    scratch = scratch[6:]
    place = Place(slabs)
    place.greet(chain=True)
    schedules, jobs, base = [], [], 0
    for i, plane0, planes in groups:
        rows, n = outs[i].shape[1:]
        parts = parts_of(rows)
        size = rows // parts
        both = []
        for p in range(parts):
            names = sum_buffers(planes, slabs, size, n, tensor, ORDERS[p])
            bufs = {name: scratch.pop(0) for name in names}
            job = PartSum(
                place, parts_in[i], outs[i].at[pl.ds(plane0, planes)],
                pl.ds(plane0, planes), pl.ds(p * size, size), n, ORDERS[p], bufs,
                (load_sem, send_sem, recv_sem), base,
            )
            base += 1
            both.append(job.ticks())
            jobs.append(job)
        length = max(len(t) for t in both)
        schedules.append([sum((t[k] for t in both if k < len(t)), []) for k in range(length)])
    schedules.append(small_sum(place, small, small_out, small_got, (small_send, small_recv)))
    merge(schedules, lag)
    for job in jobs:
        job.drain()


def sum_all(partials, small, groups, dp, tensor, lag=2):
    slabs = dp // 4
    wide, outs = [], []
    for part in partials:
        planes, rows, cols = part.shape
        wide.append(part.reshape(planes, slabs, 2, 2, rows // dp, cols))
        outs.append(jax.ShapeDtypeStruct((planes, rows // dp, cols // tensor), jnp.float32))
    scratch, bases = [], 0
    for i, _, planes in groups:
        rows, n = outs[i].shape[1:]
        parts = parts_of(rows)
        for p in range(parts):
            shapes = sum_buffers(planes, slabs, rows // parts, n, tensor, ORDERS[p])
            scratch += [pltpu.VMEM(shape, jnp.bfloat16) for shape in shapes.values()]
            bases += 1
    dma = pltpu.SemaphoreType.DMA
    vmem = pl.BlockSpec(memory_space=pltpu.VMEM)
    return pl.pallas_call(
        functools.partial(sum_kernel, slabs, tensor, groups, lag, len(partials)),
        out_shape=[*outs, jax.ShapeDtypeStruct(small.shape, jnp.float32)],
        in_specs=[pl.BlockSpec(memory_space=pl.ANY)] * len(partials) + [vmem],
        out_specs=[vmem] * (len(partials) + 1),
        scratch_shapes=[
            dma((bases, slabs)),
            dma((bases, 4, slabs + 1)),
            dma((bases, 4, slabs + 1)),
            pltpu.VMEM((3 + slabs, *small.shape), jnp.float32),
            dma((3 + slabs,)),
            dma((3 + slabs,)),
            *scratch,
        ],
        compiler_params=pltpu.CompilerParams(
            collective_id=1, has_side_effects=True, vmem_limit_bytes=67043328
        ),
        name="sum_gradients",
    )(*wide, small)


TILE = 512
AHEAD = 3


def far_first(place):
    slabs = place.slabs
    tables = []
    for a in range(slabs):
        tables.append(sorted(range(slabs), key=lambda k: (-abs(k - a), -k)))
    return [
        sum(jnp.where(place.a == a, tables[a][i], 0) for a in range(slabs)) for i in range(slabs)
    ]


class TilePart(PartSum):
    def ticks(self, order_of_slabs):
        place, order = self.place, self.order
        zi = order.index("z")
        after = "".join(reversed(order[zi + 1 :]))
        before = "".join(reversed(order[:zi]))
        slabs = place.slabs
        ticks = {}
        bind = functools.partial

        def put(t, unit, cond, action):
            ticks.setdefault(t, []).append((unit, cond, action))

        def begin(stage, slab):
            self.sends.append((None, stage, slab, None))
            return bind(self.start, stage, slab)

        for i, slab in enumerate(order_of_slabs):
            t = i + 1
            for stage in after:
                put(t, i, None, begin(stage, slab))
                put(t + 1, i, None, bind(self.take, stage, slab))
                t += 1
            if i < slabs - 1:
                up, down = slab > place.a, slab < place.a
                from_both = jnp.logical_or(
                    jnp.logical_and(up, place.has["down"]), jnp.logical_and(down, place.has["up"])
                )
                put(t, i, from_both, bind(self.take_z, slab, slab))
                for cond, to in ((up, "up"), (down, "down")):
                    put(t, i, cond, bind(self.send_z, slab, to))
                    self.sends.append((cond, "z", slab, to))
                continue
            put(t, i, place.has["down"], bind(self.take_z, slab, slab))
            put(t, i, place.has["up"], bind(self.take_z, slab, slabs))
            for stage in before:
                put(t, i, None, begin(stage, slab))
                put(t + 1, i, None, bind(self.take, stage, slab))
                t += 1
            put(t, i, None, self.finish)
        return ticks


def tile_sum_kernel(slabs, tensor, groups, a_count, b_count, out_count, *refs):
    lefts, refs = refs[:a_count], refs[a_count:]
    rights, refs = refs[:b_count], refs[b_count:]
    small, refs = refs[0], refs[1:]
    outs, small_out, refs = refs[:out_count], refs[out_count], refs[out_count + 1 :]
    send_sem, recv_sem, core_send, core_recv, small_got, small_send, small_recv = refs[:7]
    left_buf, left_sem, turned, right_buf, right_sem = refs[7:12]
    scratch = list(refs[12:])
    place = Place(slabs)
    place.greet(chain=True)
    sigma = far_first(place)
    units = [(g, i) for g in range(len(groups)) for i in range(slabs)]
    block = 4 * outs[0].shape[1]

    def left_copy(u):
        g, i = units[u]
        at = pl.ds(pl.multiple_of(sigma[i] * block, 128), block)
        return pltpu.make_async_copy(
            lefts[groups[g][0]].at[:, at], left_buf.at[u % 2], left_sem.at[u % 2]
        )

    def right_copy(g, k):
        right = rights[groups[g][1]]
        wide = right.shape[2] // TILE
        at = pl.ds(pl.multiple_of((k % wide) * TILE, TILE), TILE)
        slot = k % (AHEAD + 1)
        return pltpu.make_async_copy(
            right.at[k // wide, :, at], right_buf.at[slot], right_sem.at[slot]
        )

    def multiply(u, tile):
        g = units[u][0]
        right = rights[groups[g][1]]
        wide = right.shape[2] // TILE
        steps = right.shape[0] * wide
        left_copy(u).wait()
        if u + 1 < len(units):
            left_copy(u + 1).start()
        turned[...] = left_buf[u % 2].T

        def body(k, carry):
            right_copy(g, k).wait()

            @pl.when(k + AHEAD < steps)
            def _():
                right_copy(g, k + AHEAD).start()

            product = jnp.dot(
                turned[...], right_buf[k % (AHEAD + 1)], preferred_element_type=jnp.float32
            )
            at = pl.ds(pl.multiple_of((k % wide) * TILE, TILE), TILE)
            tile[k // wide, :, :, :, at] = product.reshape(2, 2, block // 4, TILE).astype(
                tile.dtype
            )
            return carry

        lax.fori_loop(0, steps, body, 0)
        if u + 1 < len(units):
            preload(u + 1)

    def preload(u):
        g = units[u][0]
        right = rights[groups[g][1]]
        for k in range(min(AHEAD, right.shape[0] * (right.shape[2] // TILE))):
            right_copy(g, k).start()

    schedule, jobs, base = {}, [], 0
    tiles = {}

    def put(t, rank, cond, action):
        schedule.setdefault(t, []).append((rank, cond, action))

    for g, (_, ri, oi, plane0) in enumerate(groups):
        rows, n = outs[oi].shape[1:]
        planes = rights[ri].shape[0]
        key = (planes, n)
        if key not in tiles:
            tiles[key] = scratch.pop(0)
        acc = scratch.pop(0)
        tile_pair = tiles[key]
        parts = parts_of(rows)
        size = rows // parts

        def core_copy(u, g=g, acc=acc, tile_pair=tile_pair):
            slab = sigma[units[u][1]]
            return pltpu.make_async_remote_copy(
                tile_pair.at[u % 2, :, :, 1 - place.c],
                acc.at[:, slab],
                core_send.at[g, slab],
                core_recv.at[g, slab],
                place.peer["c"],
                MESH,
            )

        def make(u, tile_pair=tile_pair, core_copy=core_copy):
            multiply(u, tile_pair.at[u % 2])
            core_copy(u).start()

        def join(u, acc=acc, tile_pair=tile_pair, core_copy=core_copy):
            copy = core_copy(u)
            copy.wait_send()
            copy.wait_recv()
            add_into(
                acc.at[:, sigma[units[u][1]]], tile_pair.at[u % 2, :, :, place.c]
            )

        for i in range(slabs):
            u = g * slabs + i
            put(u, (1, 0), None, functools.partial(make, u))
            put(u + 1, (0, 0), None, functools.partial(join, u))
        for p in range(parts):
            shapes = sum_buffers(planes, slabs, size, n, tensor, ORDERS[p])
            bufs = {name: scratch.pop(0) for name in "xyz"}
            bufs["acc"] = acc.at[:, :, :, pl.ds(p * size, size)]
            job = TilePart(
                place, None, outs[oi].at[pl.ds(plane0, planes)], None, pl.ds(p * size, size), n,
                ORDERS[p], bufs, (None, send_sem, recv_sem), base,
            )
            base += 1
            jobs.append(job)
            for t, actions in job.ticks(sigma).items():
                for k, (i, cond, action) in enumerate(actions):
                    u = g * slabs + i
                    first = t == i + 1 and getattr(action, "func", None) == job.start
                    rank = (0, 1 + p) if first else (2, -u)
                    put(g * slabs + t, rank, cond, action)
    for t, actions in enumerate(small_sum(place, small, small_out, small_got, (small_send, small_recv))):
        for cond, action in actions:
            put(t + 1, (3, 0), cond, action)
    left_copy(0).start()
    preload(0)
    for t in sorted(schedule):
        for _, cond, action in sorted(schedule[t], key=lambda item: item[0]):
            when(cond, action)
    for job in jobs:
        job.drain()


def tile_sum_all(lefts, rights, outs, groups, small, dp, tensor):
    slabs = dp // 4
    bf = jnp.bfloat16
    seen, scratch, bases = set(), [], 0
    for _, ri, oi, _ in groups:
        planes = rights[ri].shape[0]
        rows, n = outs[oi].shape[1:]
        cols = n * tensor
        if (planes, n) not in seen:
            seen.add((planes, n))
            scratch.append(pltpu.VMEM((2, planes, 2, 2, rows, cols), bf))
        scratch.append(pltpu.VMEM((planes, slabs, 2, rows, cols), bf))
        parts = parts_of(rows)
        for p in range(parts):
            shapes = sum_buffers(planes, slabs, rows // parts, n, tensor, ORDERS[p])
            scratch += [pltpu.VMEM(shapes[name], bf) for name in "xyz"]
            bases += 1
    dma = pltpu.SemaphoreType.DMA
    vmem = pl.BlockSpec(memory_space=pltpu.VMEM)
    depth = lefts[0].shape[0]
    block = 4 * outs[0].shape[1]
    return pl.pallas_call(
        functools.partial(
            tile_sum_kernel, slabs, tensor, groups, len(lefts), len(rights), len(outs)
        ),
        out_shape=[*outs, jax.ShapeDtypeStruct(small.shape, jnp.float32)],
        in_specs=[pl.BlockSpec(memory_space=pl.ANY)] * (len(lefts) + len(rights)) + [vmem],
        out_specs=[vmem] * (len(outs) + 1),
        scratch_shapes=[
            dma((bases, 4, slabs + 1)),
            dma((bases, 4, slabs + 1)),
            dma((len(groups), slabs)),
            dma((len(groups), slabs)),
            pltpu.VMEM((3 + slabs, *small.shape), jnp.float32),
            dma((3 + slabs,)),
            dma((3 + slabs,)),
            pltpu.VMEM((2, depth, block), bf),
            dma((2,)),
            pltpu.VMEM((block, depth), bf),
            pltpu.VMEM((AHEAD + 1, depth, TILE), bf),
            dma((AHEAD + 1,)),
            *scratch,
        ],
        compiler_params=pltpu.CompilerParams(
            collective_id=2, has_side_effects=True, vmem_limit_bytes=67043328
        ),
        name="sum_products",
    )(*lefts, *rights, small)


BLOCK = 256


class Forward:
    def __init__(self, refs, fulls):
        (self.tokens, self.gain_mix, self.taps, self.gain_ff, outs, scratch) = refs
        self.in_full, self.out_full, self.gate_up_full = fulls[:3]
        (self.normed_o, self.proj_o, self.gated_o, self.residual_o, self.ff_o, self.gate_o,
         self.up_o, self.hidden_o) = outs
        (self.normed, self.proj, self.mixed, self.proj_low, self.gated, self.residual, self.ff,
         self.gate, self.weight, self.first, self.second, self.load_sem, self.save_sem,
         self.first_sem, self.second_sem) = scratch
        self.rows, self.width = self.tokens.shape
        self.blocks = self.rows // BLOCK
        self.late = []

    def rows_of(self, k):
        return pl.ds(pl.multiple_of(k * BLOCK, BLOCK), BLOCK)

    def wide(self, tile):
        return pl.ds(pl.multiple_of(tile * TILE, TILE), TILE)

    def save(self, k, ref, out):
        copy = pltpu.make_async_copy(ref, out, self.save_sem.at[k])
        copy.start()
        self.late.append(copy)

    def weight_copy(self, full, plane, tile, slot):
        wide = full.shape[-1]
        matrix = full.at[plane].reshape(self.width, wide)
        return pltpu.make_async_copy(
            matrix.at[:, self.wide(tile)], self.weight.at[slot], self.load_sem.at[slot]
        )

    def norm_rows(self, source, gain, target):
        def body(k, carry):
            at = self.rows_of(k)
            values = source[at, :].astype(jnp.float32)
            scale = lax.rsqrt(jnp.mean(values * values, axis=-1, keepdims=True) + EPS)
            target[at, :] = (values * scale * gain[...]).astype(jnp.bfloat16)
            return carry

        lax.fori_loop(0, self.blocks, body, 0)

    def begin(self):
        self.norm_rows(self.tokens, self.gain_mix, self.normed)
        self.save(0, self.normed, self.normed_o)

    def channels(self, tile):
        for j in range(3):
            self.weight_copy(self.in_full, j, tile, j).start()
        if tile:
            self.late.pop().wait()
        for j in range(3):
            self.weight_copy(self.in_full, j, tile, j).wait()

            def project(k, carry, j=j):
                at = self.rows_of(k)
                product = jnp.dot(
                    self.normed[at, :], self.weight[j], preferred_element_type=jnp.float32
                )
                self.proj[j, at, :] = product
                self.proj_low[j, at, :] = product.astype(jnp.bfloat16)
                return carry

            lax.fori_loop(0, self.blocks, project, 0)
        cols = slice(tile * TILE, (tile + 1) * TILE)
        pad = 8
        for s in range(self.rows // LEN):
            self.mixed[:pad, :] = jnp.zeros((pad, TILE), jnp.float32)
            for k in range(LEN // BLOCK):
                at = slice(s * LEN + k * BLOCK, s * LEN + (k + 1) * BLOCK)
                self.mixed[pad + k * BLOCK : pad + (k + 1) * BLOCK, :] = (
                    self.proj[0, at, :] * self.proj[2, at, :]
                )
            for k in range(LEN // BLOCK):
                at = slice(s * LEN + k * BLOCK, s * LEN + (k + 1) * BLOCK)
                base = pad + k * BLOCK
                conv = (
                    self.taps[0:1, cols] * self.mixed[base - 2 : base - 2 + BLOCK, :]
                    + self.taps[1:2, cols] * self.mixed[base - 1 : base - 1 + BLOCK, :]
                    + self.taps[2:3, cols] * self.mixed[base : base + BLOCK, :]
                )
                self.gated[at, cols] = (self.proj[1, at, :] * conv).astype(jnp.bfloat16)
        self.save(1, self.proj_low, self.proj_o.at[:, :, cols])

    def mixer(self):
        tiles = self.width // TILE
        for c in range(tiles):
            self.weight_copy(self.out_full, 0, c, c).start()
        for c in range(tiles):
            self.weight_copy(self.out_full, 0, c, c).wait()

        def body(k, carry):
            at = self.rows_of(k)
            total = self.tokens[at, :].astype(jnp.float32)
            for c in range(tiles):
                total = total + lax.dot_general(
                    self.gated[at, c * TILE : (c + 1) * TILE], self.weight[c],
                    (((1,), (1,)), ((), ())), preferred_element_type=jnp.float32,
                )
            self.residual[at, :] = total
            return carry

        lax.fori_loop(0, self.blocks, body, 0)
        self.norm_rows(self.residual, self.gain_ff, self.ff)
        self.save(2, self.gated, self.gated_o)
        self.save(3, self.residual, self.residual_o)
        self.save(4, self.ff, self.ff_o)

    def hidden_tiles(self, plane, first, count):
        total = self.gate_o.shape[1] // TILE
        ahead = min(3, count)
        for k in range(ahead):
            self.weight_copy(self.gate_up_full, plane, first + k, k).start()

        def out_copies(t):
            slot = t % 2
            at = self.wide(t)
            if plane == 0:
                return [
                    pltpu.make_async_copy(
                        self.first.at[slot], self.gate_o.at[:, at], self.first_sem.at[slot]
                    )
                ]
            return [
                pltpu.make_async_copy(
                    self.first.at[slot], self.up_o.at[:, at], self.first_sem.at[slot]
                ),
                pltpu.make_async_copy(
                    self.second.at[slot], self.hidden_o.at[:, at], self.second_sem.at[slot]
                ),
            ]

        def tile_step(i, carry):
            t = first + i
            slot = t % 2

            @pl.when(i >= 2)
            def _():
                for copy in out_copies(t - 2):
                    copy.wait()

            self.weight_copy(self.gate_up_full, plane, t, i % 4).wait()

            @pl.when(i + ahead < count)
            def _():
                self.weight_copy(
                    self.gate_up_full, plane, t + ahead, (i + ahead) % 4
                ).start()

            def rows_step(k, inner):
                at = self.rows_of(k)
                product = jnp.dot(
                    self.ff[at, :], self.weight[i % 4], preferred_element_type=jnp.float32
                )
                self.first[slot, at, :] = product.astype(jnp.bfloat16)
                if plane == 0:
                    self.gate[at, self.wide(t)] = product
                else:
                    gate = self.gate[at, self.wide(t)]
                    hidden = gate * jax.nn.sigmoid(gate) * product
                    self.second[slot, at, :] = hidden.astype(jnp.bfloat16)
                return inner

            lax.fori_loop(0, self.blocks, rows_step, 0)
            for copy in out_copies(t):
                copy.start()
            return carry

        lax.fori_loop(0, count, tile_step, 0)
        for t in range(max(first, first + count - 2), first + count):
            for copy in out_copies(t):
                copy.wait()

    def pieces(self, ends):
        tiles = self.gate_o.shape[1] // TILE
        some = 3
        plan = [(0, self.begin)]
        plan += [(ends[0] + c, functools.partial(self.channels, c)) for c in range(self.width // TILE)]
        plan.append((max(ends[1], ends[0] + 2), self.mixer))
        for plane in range(2):
            for k, at in enumerate(range(0, tiles, some)):
                plan.append(
                    (ends[2 + plane] + k,
                     functools.partial(self.hidden_tiles, plane, at, min(some, tiles - at)))
                )
        return plan

    def close(self):
        for copy in self.late:
            copy.wait()


def forward_kernel(slabs, groups, starts, count, *refs):
    shards, refs = refs[:count], refs[count:]
    (tokens, gain_mix, taps, gain_ff), refs = refs[:4], refs[4:]
    fulls, refs = refs[:count], refs[count:]
    outs, refs = refs[:8], refs[8:]
    send_sem, recv_sem, own_sem = refs[:3]
    place = Place(slabs)
    local = []
    for i, (shard, full) in enumerate(zip(shards, fulls)):
        n = shard.shape[2]
        columns = pl.ds(pl.multiple_of(place.x * n, 128), n)
        own = pltpu.make_async_copy(
            shard, full.at[:, place.a, place.y, place.c, :, columns], own_sem.at[i]
        )
        own.start()
        local.append(own)
    place.greet()
    for own in local:
        own.wait()
    work = Forward((tokens, gain_mix, taps, gain_ff, outs, refs[3:]), fulls)
    ticks, drains, ends, base = {}, [], [], 0
    for g, (i, plane0, planes) in enumerate(groups):
        rows, n = shards[i].shape[1:]
        parts = parts_of(rows)
        size = rows // parts
        length = 0
        for p in range(parts):
            steps, drain = gather_ticks(
                place, fulls[i], pl.ds(plane0, planes), pl.ds(p * size, size), n,
                ORDERS[p], send_sem, recv_sem, base,
            )
            base += 1
            drains.append(drain)
            length = max(length, len(steps))
            for k, actions in enumerate(steps):
                ticks.setdefault(starts[g] + k, []).extend(actions)
        ends.append(starts[g] + length - 1)
    plan = work.pieces(ends)
    for t in range(max(ends) + 1):
        for cond, action in ticks[t]:
            when(cond, action)
        if plan and plan[0][0] <= t:
            plan.pop(0)[1]()
    for _, action in plan:
        action()
    for drain in drains:
        drain()
    work.close()


def gather_forward(shards, tokens, gain_mix, taps, gain_ff, groups, starts, dp, tensor):
    slabs = dp // 4
    shapes = [s.shape for s in shards]
    bases = len(groups) * parts_of(shapes[0][1])
    rows, width = tokens.shape
    units = shapes[2][2] * tensor
    bf, f32 = jnp.bfloat16, jnp.float32
    fulls = [
        jax.ShapeDtypeStruct((s[0], slabs, 2, 2, s[1], s[2] * tensor), bf) for s in shapes
    ]
    kept = [
        jax.ShapeDtypeStruct(shape, kind)
        for shape, kind in (
            ((rows, width), bf), ((3, rows, width), bf), ((rows, width), bf),
            ((rows, width), f32), ((rows, width), bf), ((rows, units), bf),
            ((rows, units), bf), ((rows, units), bf),
        )
    ]
    dma = pltpu.SemaphoreType.DMA
    vmem = pl.BlockSpec(memory_space=pltpu.VMEM)
    anywhere = pl.BlockSpec(memory_space=pl.ANY)
    out = pl.pallas_call(
        functools.partial(forward_kernel, slabs, groups, starts, len(shards)),
        out_shape=fulls + kept,
        in_specs=[vmem] * (len(shards) + 4),
        out_specs=[anywhere] * (len(fulls) + len(kept)),
        scratch_shapes=[
            dma((bases, 4, slabs)),
            dma((bases, 4, slabs)),
            dma((len(shards),)),
            pltpu.VMEM((rows, width), bf),
            pltpu.VMEM((3, rows, TILE), f32),
            pltpu.VMEM((8 + LEN, TILE), f32),
            pltpu.VMEM((3, rows, TILE), bf),
            pltpu.VMEM((rows, width), bf),
            pltpu.VMEM((rows, width), f32),
            pltpu.VMEM((rows, width), bf),
            pltpu.VMEM((rows, units), f32),
            pltpu.VMEM((4, width, TILE), bf),
            pltpu.VMEM((2, rows, TILE), bf),
            pltpu.VMEM((2, rows, TILE), bf),
            dma((4,)),
            dma((5,)),
            dma((2,)),
            dma((2,)),
        ],
        compiler_params=pltpu.CompilerParams(
            collective_id=0, has_side_effects=True, vmem_limit_bytes=67043328
        ),
        name="gather_forward",
    )(*shards, tokens, gain_mix[None], taps, gain_ff[None])
    count = len(shards)
    weights = [f.reshape(s[0], dp * s[1], s[2] * tensor) for f, s in zip(out[:count], shapes)]
    return weights, out[count:]


def per_device(
    tokens,
    gain_mix,
    in_weight,
    conv_weight,
    out_weight,
    gain_ff,
    gate_up_weight,
    down_weight,
    grad_out,
):
    inputs = tokens.astype(jnp.float32)
    dp, tensor = lax.axis_size("dp"), lax.axis_size("tensor")
    weights, kept = gather_forward(
        [in_weight, out_weight[None], gate_up_weight, down_weight[None]],
        tokens,
        gain_mix,
        conv_weight,
        gain_ff,
        GROUPS,
        STARTS,
        dp,
        tensor,
    )
    in_full, out_full, gate_up_full, down_full = weights
    normed_mix, projected, gated_rows, residual, normed_ff, gate_low, up_low, hidden = kept
    projected = projected.astype(jnp.float32)
    out_full, down_full = out_full[0], down_full[0]
    rows, width = tokens.shape
    seq_count = rows // LEN
    scale_mix = norm_scale(inputs)
    shaped = (seq_count, LEN, width)
    input_gate = projected[0].reshape(shaped)
    output_gate = projected[1].reshape(shaped)
    value_part = projected[2].reshape(shaped)
    mixed_in = input_gate * value_part
    conv_out = (
        conv_weight[0] * delayed(mixed_in, 2)
        + conv_weight[1] * delayed(mixed_in, 1)
        + conv_weight[2] * mixed_in
    )
    scale_ff = norm_scale(residual)
    gate_pre = gate_low.astype(jnp.float32)
    up_value = up_low.astype(jnp.float32)
    sigmoid_gate = jax.nn.sigmoid(gate_pre)
    silu_gate = gate_pre * sigmoid_gate
    block_out = (
        residual
        + lax.dot_general(
            hidden, down_full, (((1,), (1,)), ((), ())), preferred_element_type=jnp.float32
        )
    ).astype(jnp.bfloat16)
    hidden_grad = jnp.dot(grad_out, down_full, preferred_element_type=jnp.float32)
    silu_slope = sigmoid_gate * (1.0 + gate_pre * (1.0 - sigmoid_gate))
    gate_grad = (hidden_grad * up_value * silu_slope).astype(jnp.bfloat16)
    up_grad = (hidden_grad * silu_gate).astype(jnp.bfloat16)
    gate_up_grad = jnp.stack([gate_grad, up_grad])
    ffn_in_grad = jnp.einsum(
        "jgf,jdf->gd", gate_up_grad, gate_up_full, preferred_element_type=jnp.float32
    )
    residual_back, gain_ff_grad = norm_back(residual, scale_ff, gain_ff, ffn_in_grad)
    residual_grad = grad_out.astype(jnp.float32) + residual_back
    mixer_grads = residual_grad.astype(jnp.bfloat16)
    gated_grad = jnp.dot(mixer_grads, out_full, preferred_element_type=jnp.float32).reshape(shaped)
    output_gate_grad = gated_grad * conv_out
    conv_grad_in = gated_grad * output_gate
    mixed_grad = (
        conv_weight[2] * conv_grad_in
        + conv_weight[1] * advanced(conv_grad_in, 1)
        + conv_weight[0] * advanced(conv_grad_in, 2)
    )
    tap_grads = jnp.stack(
        [
            jnp.sum(conv_grad_in * delayed(mixed_in, 2), axis=(0, 1)),
            jnp.sum(conv_grad_in * delayed(mixed_in, 1), axis=(0, 1)),
            jnp.sum(conv_grad_in * mixed_in, axis=(0, 1)),
        ]
    )
    proj_grad = (
        jnp.stack([mixed_grad * value_part, output_gate_grad, mixed_grad * input_gate])
        .astype(jnp.bfloat16)
        .reshape(3, rows, width)
    )
    mixer_in_grad = jnp.einsum(
        "jgc,jdc->gd", proj_grad, in_full, preferred_element_type=jnp.float32
    )
    input_back, gain_mix_grad = norm_back(inputs, scale_mix, gain_mix, mixer_in_grad)
    input_grad = residual_grad + input_back
    small = jnp.concatenate(
        [gain_mix_grad[None], gain_ff_grad[None], tap_grads, jnp.zeros((3, width), jnp.float32)]
    )
    if in_weight.shape[1] >= 64:
        shards = (down_weight[None], gate_up_weight, in_weight, out_weight[None])
        down_sum, gate_up_sum, in_sum, out_sum, small_sums = tile_sum_all(
            [grad_out, normed_ff, normed_mix, mixer_grads],
            [hidden[None], gate_grad[None], up_grad[None], proj_grad, gated_rows[None]],
            [jax.ShapeDtypeStruct(shard.shape, jnp.float32) for shard in shards],
            PRODUCTS,
            small,
            dp,
            tensor,
        )
    else:
        down_grad = lax.dot_general(
            grad_out, hidden, (((0,), (0,)), ((), ())), preferred_element_type=jnp.float32
        )
        gate_up_weight_grad = jnp.einsum(
            "gd,jgf->jdf", normed_ff, gate_up_grad, preferred_element_type=jnp.float32
        )
        out_weight_grad = lax.dot_general(
            mixer_grads, gated_rows, (((0,), (0,)), ((), ())), preferred_element_type=jnp.float32
        )
        in_weight_grad = jnp.einsum(
            "gd,jgc->jdc", normed_mix, proj_grad, preferred_element_type=jnp.float32
        )
        down_sum, gate_up_sum, in_sum, out_sum, small_sums = sum_all(
            [
                down_grad.astype(jnp.bfloat16)[None],
                gate_up_weight_grad.astype(jnp.bfloat16),
                in_weight_grad.astype(jnp.bfloat16),
                out_weight_grad.astype(jnp.bfloat16)[None],
            ],
            small,
            SUM_GROUPS,
            dp,
            tensor,
        )
    return (
        block_out,
        input_grad,
        small_sums[0],
        in_sum,
        small_sums[2:5],
        out_sum[0],
        small_sums[1],
        gate_up_sum,
        down_sum[0],
    )


def solution(mesh):
    in_specs = (
        P(("dp", "tensor"), None),
        P(),
        P(None, "dp", "tensor"),
        P(),
        P("dp", "tensor"),
        P(),
        P(None, "dp", "tensor"),
        P("dp", "tensor"),
        P(("dp", "tensor"), None),
    )
    out_specs = (
        P(("dp", "tensor"), None),
        P(("dp", "tensor"), None),
        P(),
        P(None, "dp", "tensor"),
        P(),
        P("dp", "tensor"),
        P(),
        P(None, "dp", "tensor"),
        P("dp", "tensor"),
    )
    return jax.shard_map(
        per_device, mesh=mesh, in_specs=in_specs, out_specs=out_specs, check_vma=False
    )
```

```python
import functools

import jax
import jax.numpy as jnp
from jax import lax
from jax.experimental import pallas as pl
from jax.experimental.pallas import tpu as pltpu
from jax.sharding import PartitionSpec as P

LEN = 1024


EPS = 1e-05


def norm_scale(values):
    return lax.rsqrt(jnp.mean(values * values, axis=-1, keepdims=True) + EPS)


def delayed(values, shift_by):
    return jnp.pad(values[:, : values.shape[1] - shift_by], ((0, 0), (shift_by, 0), (0, 0)))


def advanced(values, shift_by):
    return jnp.pad(values[:, shift_by:], ((0, 0), (0, shift_by), (0, 0)))


def norm_back(values, row_scale, gain_vec, grad_normed):
    weighted = grad_normed * gain_vec
    inner_mean = jnp.mean(weighted * values, axis=-1, keepdims=True)
    grad_values = row_scale * weighted - values * row_scale**3 * inner_mean
    gain_grad = jnp.sum(grad_normed * values * row_scale, axis=0)
    return (grad_values, gain_grad)


MESH = pl.DeviceIdType.MESH
ORDERS = ("xzy", "yzx", "zxy", "zyx")
GROUPS = ((0, 0, 3), (1, 0, 1), (2, 0, 1), (2, 1, 1), (3, 0, 1))
SUM_GROUPS = ((0, 0, 1), (1, 0, 1), (1, 1, 1), (2, 0, 3), (3, 0, 1))
PRODUCTS = ((3, 4, 3, 0), (0, 0, 0, 0), (1, 1, 1, 0), (1, 2, 1, 1), (2, 3, 2, 0))
STARTS = (0, 1, 3, 6, 9)
STAGES = {"x": 0, "y": 1, "z": 2, "c": 3}


class Place:
    def __init__(self, slabs):
        dp = lax.axis_index("dp")
        self.dp, self.x = dp, lax.axis_index("tensor")
        self.slabs = slabs
        self.a = dp // 4
        self.y = (dp // 2) % 2
        self.c = dp % 2
        self.peer = {
            "x": (dp, 1 - self.x),
            "y": (dp + 2 - 4 * self.y, self.x),
            "c": (dp + 1 - 2 * self.c, self.x),
            "down": (dp - 4, self.x),
            "up": (dp + 4, self.x),
        }
        self.has = {"down": self.a > 0, "up": self.a < slabs - 1}

    def greet(self, chain=False):
        barrier = pltpu.get_barrier_semaphore()
        for name in ("x", "y", "c"):
            pl.semaphore_signal(barrier, 1, device_id=self.peer[name], device_id_type=MESH)
        if chain:
            for slab in range(self.slabs):

                @pl.when(slab != self.a)
                def _(slab=slab):
                    pl.semaphore_signal(
                        barrier,
                        1,
                        device_id=(self.dp + 4 * (slab - self.a), self.x),
                        device_id_type=MESH,
                    )

            pl.semaphore_wait(barrier, 2 + self.slabs)
            return
        for name in ("down", "up"):

            @pl.when(self.has[name])
            def _(name=name):
                pl.semaphore_signal(barrier, 1, device_id=self.peer[name], device_id_type=MESH)

        ends = self.has["down"].astype(jnp.int32) + self.has["up"].astype(jnp.int32)
        pl.semaphore_wait(barrier, 3 + ends)


def pick(own, which):
    if which == "all":
        return slice(None)
    return own if which == "own" else 1 - own


def gather_ticks(place, full, planes, rows, cols, order, send_sem, recv_sem, base):
    here = place
    n = cols

    def region(slab, y, c, x):
        columns = slice(None) if x == "all" else pl.ds(pl.multiple_of(pick(here.x, x) * n, 128), n)
        return full.at[planes, slab, pick(here.y, y), pick(here.c, c), rows, columns]

    def span(stage, side):
        i = order.index(stage) if stage != "c" else 3
        done = order[:i]
        sel = {d: ("all" if d in done else "own") for d in "xy"}
        if stage in "xy":
            sel[stage] = side
        return sel["y"], (side if stage == "c" else "own"), sel["x"]

    def copy(stage, slab, side, peer):
        ref = region(slab, *span(stage, side))
        k = STAGES[stage]
        return pltpu.make_async_remote_copy(
            ref, ref, send_sem.at[base, k, slab], recv_sem.at[base, k, slab], peer, MESH
        )

    zi = order.index("z")
    pre, post = order[:zi], order[zi + 1 :] + "c"
    total = len(pre) + here.slabs + len(post) + 1
    ticks = [[] for _ in range(total)]
    sends = []

    def start(stage, slab, peer):
        copy(stage, slab, "own", peer).start()

    def finish(stage, slab):
        copy(stage, slab, "own" if stage == "z" else "other", here.peer["x"]).wait_recv()

    def chain(t, stages, slab, cond):
        for i, stage in enumerate(stages):
            ticks[t + i].append((cond, functools.partial(start, stage, slab, here.peer[stage])))
            ticks[t + i + 1].append((cond, functools.partial(finish, stage, slab)))
            sends.append((cond, stage, slab))

    chain(0, pre, here.a, None)
    t0 = len(pre)
    for name in ("down", "up"):
        ticks[t0].append((here.has[name], functools.partial(start, "z", here.a, here.peer[name])))
        sends.append((here.has[name], "z", here.a))
    chain(t0, post, here.a, None)
    for s in range(1, here.slabs):
        for slab, come, to in (
            (here.a - s, here.a >= s, "up"),
            (here.a + s, here.a + s < here.slabs, "down"),
        ):
            both = jnp.logical_and(come, here.has[to])
            ticks[t0 + s].append((come, functools.partial(finish, "z", slab)))
            ticks[t0 + s].append((both, functools.partial(start, "z", slab, here.peer[to])))
            sends.append((both, "z", slab))
            chain(t0 + s, post, slab, come)

    def drain():
        for cond, stage, slab in sends:
            when(cond, copy(stage, slab, "own", here.peer["x"]).wait_send)

    return ticks, drain


def when(cond, action):
    if cond is None:
        action()
    else:
        pl.when(cond)(action)


def merge(schedules, lag):
    longest = max(lag * i + len(s) for i, s in enumerate(schedules))
    for t in range(longest):
        for i, s in enumerate(schedules):
            k = t - lag * i
            if 0 <= k < len(s):
                for cond, action in s[k]:
                    when(cond, action)


def parts_of(rows):
    return 4 if rows >= 64 else 1


def add_into(target, extra):
    lead = target.shape[:-2]
    count = 1
    for d in lead:
        count *= d
    for k in range(count):
        at = []
        for d in reversed(lead):
            at.insert(0, k % d)
            k = k // d
        target[tuple(at)] = target[tuple(at)] + extra[tuple(at)]


class PartSum:
    def __init__(self, place, src, out, planes, rows, n, order, bufs, sems, base):
        self.place, self.src, self.out = place, src, out
        self.planes, self.rows, self.n, self.order = planes, rows, n, order
        self.acc, self.got = bufs["acc"], bufs
        self.load_sem, self.send_sem, self.recv_sem = sems
        self.base = base
        self.sends = []

    def cut(self, ref, slab, y, x):
        place = self.place
        y = slice(None) if y == "all" else pl.ds(pick(place.y, y), 1)
        n = self.n
        x = slice(None) if x == "all" else pl.ds(pl.multiple_of(pick(place.x, x) * n, 128), n)
        return ref.at[:, slab, y, :, x]

    def span(self, stage, side):
        i = self.order.index(stage)
        sel = {d: ("all" if d in self.order[:i] else "own") for d in "xy"}
        if stage in "xy":
            sel[stage] = side
        return sel["y"], sel["x"]

    def load(self, slab):
        return pltpu.make_async_copy(
            self.src.at[self.planes, slab, :, self.place.c, self.rows, :],
            self.acc.at[:, slab],
            self.load_sem.at[self.base, slab],
        )

    def copy(self, stage, slab, peer, slot=None):
        k = STAGES[stage]
        slot = slab if slot is None else slot
        if stage == "c":
            ref = self.src.at[self.planes, slab, :, 1 - self.place.c, self.rows, :]
        else:
            ref = self.cut(self.acc, slab, *self.span(stage, "other"))
        into = self.got[stage]
        into = into.at[:, 0] if (stage != "c" and "z" in self.order[self.order.index(stage) :][1:]) else into.at[:, slot]
        return pltpu.make_async_remote_copy(
            ref, into, self.send_sem.at[self.base, k, slot], self.recv_sem.at[self.base, k, slot],
            peer, MESH,
        )

    def start(self, stage, slab):
        self.copy(stage, slab, self.place.peer[stage]).start()

    def begin(self, slab):
        self.load(slab).start()
        self.start("c", slab)

    def take(self, stage, slab, slot=None):
        copy = self.copy(stage, slab, self.place.peer["x"], slot)
        copy.wait_recv()
        slot = slab if slot is None else slot
        if stage == "c":
            self.load(slab).wait()
            add_into(self.acc.at[:, slab], self.got["c"].at[:, slot])
            return
        first = "z" in self.order[self.order.index(stage) :][1:]
        add_into(
            self.cut(self.acc, slab, *self.span(stage, "own")),
            self.got[stage].at[:, 0 if first else slot],
        )

    def take_z(self, slab, slot):
        self.take("z", slab, slot)

    def send_z(self, slab, to):
        place = self.place
        target = place.a + (1 if to == "up" else -1)
        slot = slab if to == "up" else jnp.where(slab == target, place.slabs, slab)
        self.copy("z", slab, place.peer[to], slot).start()

    def finish(self):
        place = self.place
        y, x = "own", "own"
        rows = self.rows
        self.out[:, rows, :] = self.cut(self.acc, place.a, y, x)[:, 0].astype(jnp.float32)

    def ticks(self):
        place, order = self.place, self.order
        zi = order.index("z")
        after = "c" + "".join(reversed(order[zi + 1 :]))
        before = "".join(reversed(order[:zi]))
        slabs = place.slabs
        ticks = [[] for _ in range(slabs + len(after) + len(before) + 2)]
        bind = functools.partial

        def early(t, slab, cond):
            ticks[t].append((cond, bind(self.begin, slab)))
            self.sends.append((cond, "c", slab, None))
            for i, stage in enumerate(after):
                ticks[t + i + 1].append((cond, bind(self.take, stage, slab)))
                if i + 1 < len(after):
                    ticks[t + i + 1].append((cond, bind(self.start, after[i + 1], slab)))
                    self.sends.append((cond, after[i + 1], slab, None))

        z0 = len(after)
        for k, s in enumerate(range(slabs - 1, 0, -1)):
            for slab, cond, to, more in (
                (place.a + s, place.a + s < slabs, "up", place.has["down"]),
                (place.a - s, place.a >= s, "down", place.has["up"]),
            ):
                early(k, slab, cond)
                both = jnp.logical_and(cond, more)
                ticks[z0 + k].append((both, bind(self.take_z, slab, slab)))
                ticks[z0 + k].append((cond, bind(self.send_z, slab, to)))
                self.sends.append((cond, "z", slab, to))
        last = slabs - 1
        early(last, place.a, None)
        ticks[z0 + last].append((place.has["down"], bind(self.take_z, place.a, place.a)))
        ticks[z0 + last].append((place.has["up"], bind(self.take_z, place.a, slabs)))
        t = z0 + last
        for stage in before:
            ticks[t].append((None, bind(self.start, stage, place.a)))
            self.sends.append((None, stage, place.a, None))
            ticks[t + 1].append((None, bind(self.take, stage, place.a)))
            t += 1
        ticks[t].append((None, self.finish))
        return ticks

    def drain(self):
        place = self.place
        for cond, stage, slab, to in self.sends:
            slot = None
            if to == "down":
                slot = jnp.where(slab == place.a - 1, place.slabs, slab)
            when(cond, self.copy(stage, slab, place.peer["x"], slot).wait_send)


def sum_buffers(planes, slabs, size, n, tensor, order):
    cols = n * tensor
    shapes = {"acc": (planes, slabs, 2, size, cols), "c": (planes, slabs, 2, size, cols)}
    for i, d in enumerate(order):
        ys = 2 if "y" in order[:i] else 1
        xs = cols if "x" in order[:i] else n
        count = slabs + 1 if d == "z" else (1 if "z" in order[i + 1 :] else slabs)
        shapes[d] = (planes, count, ys, size, xs)
    return shapes


def small_sum(place, mine, total, got, sems):
    send_sem, recv_sem = sems
    steps = []

    def exchange(k, name):
        return pltpu.make_async_remote_copy(
            total, got.at[k], send_sem.at[k], recv_sem.at[k], place.peer[name], MESH
        )

    def open_(k, name):
        exchange(k, name).start()

    def close(k, name):
        copy = exchange(k, name)
        copy.wait_send()
        copy.wait_recv()
        total[...] = total[...] + got[k]

    def begin():
        total[...] = mine[...]

    def chain(slab):
        return pltpu.make_async_remote_copy(
            total, got.at[3 + place.a], send_sem.at[3 + slab], recv_sem.at[3 + place.a],
            (place.dp + 4 * (slab - place.a), place.x), MESH,
        )

    def arrival(slab):
        return pltpu.make_async_remote_copy(
            total, got.at[3 + slab], send_sem.at[3 + slab], recv_sem.at[3 + slab],
            (place.dp, place.x), MESH,
        )

    def spread():
        for slab in range(place.slabs):
            pl.when(slab != place.a)(lambda slab=slab: chain(slab).start())

    def collect():
        for slab in range(place.slabs):

            def wait(slab=slab):
                chain(slab).wait_send()
                arrival(slab).wait_recv()

            pl.when(slab != place.a)(wait)
        got[3 + place.a] = total[...]
        value = got[3]
        for slab in range(1, place.slabs):
            value = value + got[3 + slab]
        total[...] = value

    names = "cxy"
    steps.append([begin, functools.partial(open_, 0, "c")])
    for k, name in enumerate(names):
        then = functools.partial(open_, k + 1, names[k + 1]) if k < 2 else spread
        steps.append([functools.partial(close, k, name), then])
    steps.append([collect])
    return [[(None, action) for action in step] for step in steps]


def sum_kernel(slabs, tensor, groups, lag, count, *refs):
    parts_in, small = refs[:count], refs[count]
    outs, small_out = refs[count + 1 : 2 * count + 1], refs[2 * count + 1]
    scratch = list(refs[2 * count + 2 :])
    load_sem, send_sem, recv_sem, small_got, small_send, small_recv = scratch[:6]
    scratch = scratch[6:]
    place = Place(slabs)
    place.greet(chain=True)
    schedules, jobs, base = [], [], 0
    for i, plane0, planes in groups:
        rows, n = outs[i].shape[1:]
        parts = parts_of(rows)
        size = rows // parts
        both = []
        for p in range(parts):
            names = sum_buffers(planes, slabs, size, n, tensor, ORDERS[p])
            bufs = {name: scratch.pop(0) for name in names}
            job = PartSum(
                place, parts_in[i], outs[i].at[pl.ds(plane0, planes)],
                pl.ds(plane0, planes), pl.ds(p * size, size), n, ORDERS[p], bufs,
                (load_sem, send_sem, recv_sem), base,
            )
            base += 1
            both.append(job.ticks())
            jobs.append(job)
        length = max(len(t) for t in both)
        schedules.append([sum((t[k] for t in both if k < len(t)), []) for k in range(length)])
    schedules.append(small_sum(place, small, small_out, small_got, (small_send, small_recv)))
    merge(schedules, lag)
    for job in jobs:
        job.drain()


def sum_all(partials, small, groups, dp, tensor, lag=2):
    slabs = dp // 4
    wide, outs = [], []
    for part in partials:
        planes, rows, cols = part.shape
        wide.append(part.reshape(planes, slabs, 2, 2, rows // dp, cols))
        outs.append(jax.ShapeDtypeStruct((planes, rows // dp, cols // tensor), jnp.float32))
    scratch, bases = [], 0
    for i, _, planes in groups:
        rows, n = outs[i].shape[1:]
        parts = parts_of(rows)
        for p in range(parts):
            shapes = sum_buffers(planes, slabs, rows // parts, n, tensor, ORDERS[p])
            scratch += [pltpu.VMEM(shape, jnp.bfloat16) for shape in shapes.values()]
            bases += 1
    dma = pltpu.SemaphoreType.DMA
    vmem = pl.BlockSpec(memory_space=pltpu.VMEM)
    return pl.pallas_call(
        functools.partial(sum_kernel, slabs, tensor, groups, lag, len(partials)),
        out_shape=[*outs, jax.ShapeDtypeStruct(small.shape, jnp.float32)],
        in_specs=[pl.BlockSpec(memory_space=pl.ANY)] * len(partials) + [vmem],
        out_specs=[vmem] * (len(partials) + 1),
        scratch_shapes=[
            dma((bases, slabs)),
            dma((bases, 4, slabs + 1)),
            dma((bases, 4, slabs + 1)),
            pltpu.VMEM((3 + slabs, *small.shape), jnp.float32),
            dma((3 + slabs,)),
            dma((3 + slabs,)),
            *scratch,
        ],
        compiler_params=pltpu.CompilerParams(
            collective_id=1, has_side_effects=True, vmem_limit_bytes=67043328
        ),
        name="sum_gradients",
    )(*wide, small)


TILE = 512
AHEAD = 3


def far_first(place):
    slabs = place.slabs
    tables = []
    for a in range(slabs):
        tables.append(sorted(range(slabs), key=lambda k: (-abs(k - a), -k)))
    return [
        sum(jnp.where(place.a == a, tables[a][i], 0) for a in range(slabs)) for i in range(slabs)
    ]


class TilePart(PartSum):
    def ticks(self, order_of_slabs):
        place, order = self.place, self.order
        zi = order.index("z")
        after = "".join(reversed(order[zi + 1 :]))
        before = "".join(reversed(order[:zi]))
        slabs = place.slabs
        ticks = {}
        bind = functools.partial

        def put(t, unit, cond, action):
            ticks.setdefault(t, []).append((unit, cond, action))

        def begin(stage, slab):
            self.sends.append((None, stage, slab, None))
            return bind(self.start, stage, slab)

        for i, slab in enumerate(order_of_slabs):
            t = i + 1
            for stage in after:
                put(t, i, None, begin(stage, slab))
                put(t + 1, i, None, bind(self.take, stage, slab))
                t += 1
            if i < slabs - 1:
                up, down = slab > place.a, slab < place.a
                from_both = jnp.logical_or(
                    jnp.logical_and(up, place.has["down"]), jnp.logical_and(down, place.has["up"])
                )
                put(t, i, from_both, bind(self.take_z, slab, slab))
                for cond, to in ((up, "up"), (down, "down")):
                    put(t, i, cond, bind(self.send_z, slab, to))
                    self.sends.append((cond, "z", slab, to))
                continue
            put(t, i, place.has["down"], bind(self.take_z, slab, slab))
            put(t, i, place.has["up"], bind(self.take_z, slab, slabs))
            for stage in before:
                put(t, i, None, begin(stage, slab))
                put(t + 1, i, None, bind(self.take, stage, slab))
                t += 1
            put(t, i, None, self.finish)
        return ticks


def tile_sum_kernel(slabs, tensor, groups, a_count, b_count, out_count, *refs):
    lefts, refs = refs[:a_count], refs[a_count:]
    rights, refs = refs[:b_count], refs[b_count:]
    small, refs = refs[0], refs[1:]
    outs, small_out, refs = refs[:out_count], refs[out_count], refs[out_count + 1 :]
    send_sem, recv_sem, core_send, core_recv, small_got, small_send, small_recv = refs[:7]
    left_buf, left_sem, turned, right_buf, right_sem = refs[7:12]
    scratch = list(refs[12:])
    place = Place(slabs)
    place.greet(chain=True)
    sigma = far_first(place)
    units = [(g, i) for g in range(len(groups)) for i in range(slabs)]
    block = 4 * outs[0].shape[1]

    def left_copy(u):
        g, i = units[u]
        at = pl.ds(pl.multiple_of(sigma[i] * block, 128), block)
        return pltpu.make_async_copy(
            lefts[groups[g][0]].at[:, at], left_buf.at[u % 2], left_sem.at[u % 2]
        )

    def right_copy(g, k):
        right = rights[groups[g][1]]
        wide = right.shape[2] // TILE
        at = pl.ds(pl.multiple_of((k % wide) * TILE, TILE), TILE)
        slot = k % (AHEAD + 1)
        return pltpu.make_async_copy(
            right.at[k // wide, :, at], right_buf.at[slot], right_sem.at[slot]
        )

    def multiply(u, tile):
        g = units[u][0]
        right = rights[groups[g][1]]
        wide = right.shape[2] // TILE
        steps = right.shape[0] * wide
        left_copy(u).wait()
        if u + 1 < len(units):
            left_copy(u + 1).start()
        turned[...] = left_buf[u % 2].T

        def body(k, carry):
            right_copy(g, k).wait()

            @pl.when(k + AHEAD < steps)
            def _():
                right_copy(g, k + AHEAD).start()

            product = jnp.dot(
                turned[...], right_buf[k % (AHEAD + 1)], preferred_element_type=jnp.float32
            )
            at = pl.ds(pl.multiple_of((k % wide) * TILE, TILE), TILE)
            tile[k // wide, :, :, :, at] = product.reshape(2, 2, block // 4, TILE).astype(
                tile.dtype
            )
            return carry

        lax.fori_loop(0, steps, body, 0)
        if u + 1 < len(units):
            preload(u + 1)

    def preload(u):
        g = units[u][0]
        right = rights[groups[g][1]]
        for k in range(min(AHEAD, right.shape[0] * (right.shape[2] // TILE))):
            right_copy(g, k).start()

    schedule, jobs, base = {}, [], 0
    tiles = {}

    def put(t, rank, cond, action):
        schedule.setdefault(t, []).append((rank, cond, action))

    for g, (_, ri, oi, plane0) in enumerate(groups):
        rows, n = outs[oi].shape[1:]
        planes = rights[ri].shape[0]
        key = (planes, n)
        if key not in tiles:
            tiles[key] = scratch.pop(0)
        acc = scratch.pop(0)
        tile_pair = tiles[key]
        parts = parts_of(rows)
        size = rows // parts

        def core_copy(u, g=g, acc=acc, tile_pair=tile_pair):
            slab = sigma[units[u][1]]
            return pltpu.make_async_remote_copy(
                tile_pair.at[u % 2, :, :, 1 - place.c],
                acc.at[:, slab],
                core_send.at[g, slab],
                core_recv.at[g, slab],
                place.peer["c"],
                MESH,
            )

        def make(u, tile_pair=tile_pair, core_copy=core_copy):
            multiply(u, tile_pair.at[u % 2])
            core_copy(u).start()

        def join(u, acc=acc, tile_pair=tile_pair, core_copy=core_copy):
            copy = core_copy(u)
            copy.wait_send()
            copy.wait_recv()
            add_into(
                acc.at[:, sigma[units[u][1]]], tile_pair.at[u % 2, :, :, place.c]
            )

        for i in range(slabs):
            u = g * slabs + i
            put(u, (-1, 0), None, functools.partial(make, u))
            put(u + 1, (0, 0), None, functools.partial(join, u))
        for p in range(parts):
            shapes = sum_buffers(planes, slabs, size, n, tensor, ORDERS[p])
            bufs = {name: scratch.pop(0) for name in "xyz"}
            bufs["acc"] = acc.at[:, :, :, pl.ds(p * size, size)]
            job = TilePart(
                place, None, outs[oi].at[pl.ds(plane0, planes)], None, pl.ds(p * size, size), n,
                ORDERS[p], bufs, (None, send_sem, recv_sem), base,
            )
            base += 1
            jobs.append(job)
            for t, actions in job.ticks(sigma).items():
                for k, (i, cond, action) in enumerate(actions):
                    u = g * slabs + i
                    first = t == i + 1 and getattr(action, "func", None) == job.start
                    rank = (0, 1 + p) if first else (2, -u)
                    put(g * slabs + t, rank, cond, action)
    for t, actions in enumerate(small_sum(place, small, small_out, small_got, (small_send, small_recv))):
        for cond, action in actions:
            put(t + 1, (3, 0), cond, action)
    left_copy(0).start()
    preload(0)
    for t in sorted(schedule):
        for _, cond, action in sorted(schedule[t], key=lambda item: item[0]):
            when(cond, action)
    for job in jobs:
        job.drain()


def tile_sum_all(lefts, rights, outs, groups, small, dp, tensor):
    slabs = dp // 4
    bf = jnp.bfloat16
    seen, scratch, bases = set(), [], 0
    for _, ri, oi, _ in groups:
        planes = rights[ri].shape[0]
        rows, n = outs[oi].shape[1:]
        cols = n * tensor
        if (planes, n) not in seen:
            seen.add((planes, n))
            scratch.append(pltpu.VMEM((2, planes, 2, 2, rows, cols), bf))
        scratch.append(pltpu.VMEM((planes, slabs, 2, rows, cols), bf))
        parts = parts_of(rows)
        for p in range(parts):
            shapes = sum_buffers(planes, slabs, rows // parts, n, tensor, ORDERS[p])
            scratch += [pltpu.VMEM(shapes[name], bf) for name in "xyz"]
            bases += 1
    dma = pltpu.SemaphoreType.DMA
    vmem = pl.BlockSpec(memory_space=pltpu.VMEM)
    depth = lefts[0].shape[0]
    block = 4 * outs[0].shape[1]
    return pl.pallas_call(
        functools.partial(
            tile_sum_kernel, slabs, tensor, groups, len(lefts), len(rights), len(outs)
        ),
        out_shape=[*outs, jax.ShapeDtypeStruct(small.shape, jnp.float32)],
        in_specs=[pl.BlockSpec(memory_space=pl.ANY)] * (len(lefts) + len(rights)) + [vmem],
        out_specs=[vmem] * (len(outs) + 1),
        scratch_shapes=[
            dma((bases, 4, slabs + 1)),
            dma((bases, 4, slabs + 1)),
            dma((len(groups), slabs)),
            dma((len(groups), slabs)),
            pltpu.VMEM((3 + slabs, *small.shape), jnp.float32),
            dma((3 + slabs,)),
            dma((3 + slabs,)),
            pltpu.VMEM((2, depth, block), bf),
            dma((2,)),
            pltpu.VMEM((block, depth), bf),
            pltpu.VMEM((AHEAD + 1, depth, TILE), bf),
            dma((AHEAD + 1,)),
            *scratch,
        ],
        compiler_params=pltpu.CompilerParams(
            collective_id=2, has_side_effects=True, vmem_limit_bytes=67043328
        ),
        name="sum_products",
    )(*lefts, *rights, small)


BLOCK = 256


class Forward:
    def __init__(self, refs, fulls):
        (self.tokens, self.gain_mix, self.taps, self.gain_ff, outs, scratch) = refs
        self.in_full, self.out_full, self.gate_up_full = fulls[:3]
        (self.normed_o, self.proj_o, self.gated_o, self.residual_o, self.ff_o, self.gate_o,
         self.up_o, self.hidden_o) = outs
        (self.normed, self.proj, self.mixed, self.proj_low, self.gated, self.residual, self.ff,
         self.gate, self.weight, self.first, self.second, self.load_sem, self.save_sem,
         self.first_sem, self.second_sem) = scratch
        self.rows, self.width = self.tokens.shape
        self.blocks = self.rows // BLOCK
        self.late = []

    def rows_of(self, k):
        return pl.ds(pl.multiple_of(k * BLOCK, BLOCK), BLOCK)

    def wide(self, tile):
        return pl.ds(pl.multiple_of(tile * TILE, TILE), TILE)

    def save(self, k, ref, out):
        copy = pltpu.make_async_copy(ref, out, self.save_sem.at[k])
        copy.start()
        self.late.append(copy)

    def weight_copy(self, full, plane, tile, slot):
        wide = full.shape[-1]
        matrix = full.at[plane].reshape(self.width, wide)
        return pltpu.make_async_copy(
            matrix.at[:, self.wide(tile)], self.weight.at[slot], self.load_sem.at[slot]
        )

    def norm_rows(self, source, gain, target):
        def body(k, carry):
            at = self.rows_of(k)
            values = source[at, :].astype(jnp.float32)
            scale = lax.rsqrt(jnp.mean(values * values, axis=-1, keepdims=True) + EPS)
            target[at, :] = (values * scale * gain[...]).astype(jnp.bfloat16)
            return carry

        lax.fori_loop(0, self.blocks, body, 0)

    def begin(self):
        self.norm_rows(self.tokens, self.gain_mix, self.normed)
        self.save(0, self.normed, self.normed_o)

    def channels(self, tile):
        for j in range(3):
            self.weight_copy(self.in_full, j, tile, j).start()
        if tile:
            self.late.pop().wait()
        for j in range(3):
            self.weight_copy(self.in_full, j, tile, j).wait()

            def project(k, carry, j=j):
                at = self.rows_of(k)
                product = jnp.dot(
                    self.normed[at, :], self.weight[j], preferred_element_type=jnp.float32
                )
                self.proj[j, at, :] = product
                self.proj_low[j, at, :] = product.astype(jnp.bfloat16)
                return carry

            lax.fori_loop(0, self.blocks, project, 0)
        cols = slice(tile * TILE, (tile + 1) * TILE)
        pad = 8
        for s in range(self.rows // LEN):
            self.mixed[:pad, :] = jnp.zeros((pad, TILE), jnp.float32)
            for k in range(LEN // BLOCK):
                at = slice(s * LEN + k * BLOCK, s * LEN + (k + 1) * BLOCK)
                self.mixed[pad + k * BLOCK : pad + (k + 1) * BLOCK, :] = (
                    self.proj[0, at, :] * self.proj[2, at, :]
                )
            for k in range(LEN // BLOCK):
                at = slice(s * LEN + k * BLOCK, s * LEN + (k + 1) * BLOCK)
                base = pad + k * BLOCK
                conv = (
                    self.taps[0:1, cols] * self.mixed[base - 2 : base - 2 + BLOCK, :]
                    + self.taps[1:2, cols] * self.mixed[base - 1 : base - 1 + BLOCK, :]
                    + self.taps[2:3, cols] * self.mixed[base : base + BLOCK, :]
                )
                self.gated[at, cols] = (self.proj[1, at, :] * conv).astype(jnp.bfloat16)
        self.save(1, self.proj_low, self.proj_o.at[:, :, cols])

    def mixer(self):
        tiles = self.width // TILE
        for c in range(tiles):
            self.weight_copy(self.out_full, 0, c, c).start()
        for c in range(tiles):
            self.weight_copy(self.out_full, 0, c, c).wait()

        def body(k, carry):
            at = self.rows_of(k)
            total = self.tokens[at, :].astype(jnp.float32)
            for c in range(tiles):
                total = total + lax.dot_general(
                    self.gated[at, c * TILE : (c + 1) * TILE], self.weight[c],
                    (((1,), (1,)), ((), ())), preferred_element_type=jnp.float32,
                )
            self.residual[at, :] = total
            return carry

        lax.fori_loop(0, self.blocks, body, 0)
        self.norm_rows(self.residual, self.gain_ff, self.ff)
        self.save(2, self.gated, self.gated_o)
        self.save(3, self.residual, self.residual_o)
        self.save(4, self.ff, self.ff_o)

    def hidden_tiles(self, plane, first, count):
        total = self.gate_o.shape[1] // TILE
        ahead = min(3, count)
        for k in range(ahead):
            self.weight_copy(self.gate_up_full, plane, first + k, k).start()

        def out_copies(t):
            slot = t % 2
            at = self.wide(t)
            if plane == 0:
                return [
                    pltpu.make_async_copy(
                        self.first.at[slot], self.gate_o.at[:, at], self.first_sem.at[slot]
                    )
                ]
            return [
                pltpu.make_async_copy(
                    self.first.at[slot], self.up_o.at[:, at], self.first_sem.at[slot]
                ),
                pltpu.make_async_copy(
                    self.second.at[slot], self.hidden_o.at[:, at], self.second_sem.at[slot]
                ),
            ]

        def tile_step(i, carry):
            t = first + i
            slot = t % 2

            @pl.when(i >= 2)
            def _():
                for copy in out_copies(t - 2):
                    copy.wait()

            self.weight_copy(self.gate_up_full, plane, t, i % 4).wait()

            @pl.when(i + ahead < count)
            def _():
                self.weight_copy(
                    self.gate_up_full, plane, t + ahead, (i + ahead) % 4
                ).start()

            def rows_step(k, inner):
                at = self.rows_of(k)
                product = jnp.dot(
                    self.ff[at, :], self.weight[i % 4], preferred_element_type=jnp.float32
                )
                self.first[slot, at, :] = product.astype(jnp.bfloat16)
                if plane == 0:
                    self.gate[at, self.wide(t)] = product
                else:
                    gate = self.gate[at, self.wide(t)]
                    hidden = gate * jax.nn.sigmoid(gate) * product
                    self.second[slot, at, :] = hidden.astype(jnp.bfloat16)
                return inner

            lax.fori_loop(0, self.blocks, rows_step, 0)
            for copy in out_copies(t):
                copy.start()
            return carry

        lax.fori_loop(0, count, tile_step, 0)
        for t in range(max(first, first + count - 2), first + count):
            for copy in out_copies(t):
                copy.wait()

    def pieces(self, ends):
        tiles = self.gate_o.shape[1] // TILE
        some = 5
        plan = [(0, self.begin)]
        plan += [(ends[0] + c, functools.partial(self.channels, c)) for c in range(self.width // TILE)]
        plan.append((max(ends[1], ends[0] + 2), self.mixer))
        for plane in range(2):
            for k, at in enumerate(range(0, tiles, some)):
                plan.append(
                    (ends[2 + plane] + k,
                     functools.partial(self.hidden_tiles, plane, at, min(some, tiles - at)))
                )
        return plan

    def close(self):
        for copy in self.late:
            copy.wait()


def forward_kernel(slabs, groups, starts, count, *refs):
    shards, refs = refs[:count], refs[count:]
    (tokens, gain_mix, taps, gain_ff), refs = refs[:4], refs[4:]
    fulls, refs = refs[:count], refs[count:]
    outs, refs = refs[:8], refs[8:]
    send_sem, recv_sem, own_sem = refs[:3]
    place = Place(slabs)
    local = []
    for i, (shard, full) in enumerate(zip(shards, fulls)):
        n = shard.shape[2]
        columns = pl.ds(pl.multiple_of(place.x * n, 128), n)
        own = pltpu.make_async_copy(
            shard, full.at[:, place.a, place.y, place.c, :, columns], own_sem.at[i]
        )
        own.start()
        local.append(own)
    place.greet()
    for own in local:
        own.wait()
    work = Forward((tokens, gain_mix, taps, gain_ff, outs, refs[3:]), fulls)
    ticks, drains, ends, base = {}, [], [], 0
    for g, (i, plane0, planes) in enumerate(groups):
        rows, n = shards[i].shape[1:]
        parts = parts_of(rows)
        size = rows // parts
        length = 0
        for p in range(parts):
            steps, drain = gather_ticks(
                place, fulls[i], pl.ds(plane0, planes), pl.ds(p * size, size), n,
                ORDERS[p], send_sem, recv_sem, base,
            )
            base += 1
            drains.append(drain)
            length = max(length, len(steps))
            for k, actions in enumerate(steps):
                ticks.setdefault(starts[g] + k, []).extend(actions)
        ends.append(starts[g] + length - 1)
    plan = work.pieces(ends)
    for t in range(max(ends) + 1):
        for cond, action in ticks[t]:
            when(cond, action)
        if plan and plan[0][0] <= t:
            plan.pop(0)[1]()
    for _, action in plan:
        action()
    for drain in drains:
        drain()
    work.close()


def gather_forward(shards, tokens, gain_mix, taps, gain_ff, groups, starts, dp, tensor):
    slabs = dp // 4
    shapes = [s.shape for s in shards]
    bases = len(groups) * parts_of(shapes[0][1])
    rows, width = tokens.shape
    units = shapes[2][2] * tensor
    bf, f32 = jnp.bfloat16, jnp.float32
    fulls = [
        jax.ShapeDtypeStruct((s[0], slabs, 2, 2, s[1], s[2] * tensor), bf) for s in shapes
    ]
    kept = [
        jax.ShapeDtypeStruct(shape, kind)
        for shape, kind in (
            ((rows, width), bf), ((3, rows, width), bf), ((rows, width), bf),
            ((rows, width), f32), ((rows, width), bf), ((rows, units), bf),
            ((rows, units), bf), ((rows, units), bf),
        )
    ]
    dma = pltpu.SemaphoreType.DMA
    vmem = pl.BlockSpec(memory_space=pltpu.VMEM)
    anywhere = pl.BlockSpec(memory_space=pl.ANY)
    out = pl.pallas_call(
        functools.partial(forward_kernel, slabs, groups, starts, len(shards)),
        out_shape=fulls + kept,
        in_specs=[vmem] * (len(shards) + 4),
        out_specs=[anywhere] * (len(fulls) + len(kept)),
        scratch_shapes=[
            dma((bases, 4, slabs)),
            dma((bases, 4, slabs)),
            dma((len(shards),)),
            pltpu.VMEM((rows, width), bf),
            pltpu.VMEM((3, rows, TILE), f32),
            pltpu.VMEM((8 + LEN, TILE), f32),
            pltpu.VMEM((3, rows, TILE), bf),
            pltpu.VMEM((rows, width), bf),
            pltpu.VMEM((rows, width), f32),
            pltpu.VMEM((rows, width), bf),
            pltpu.VMEM((rows, units), f32),
            pltpu.VMEM((4, width, TILE), bf),
            pltpu.VMEM((2, rows, TILE), bf),
            pltpu.VMEM((2, rows, TILE), bf),
            dma((4,)),
            dma((5,)),
            dma((2,)),
            dma((2,)),
        ],
        compiler_params=pltpu.CompilerParams(
            collective_id=0, has_side_effects=True, vmem_limit_bytes=67043328
        ),
        name="gather_forward",
    )(*shards, tokens, gain_mix[None], taps, gain_ff[None])
    count = len(shards)
    weights = [f.reshape(s[0], dp * s[1], s[2] * tensor) for f, s in zip(out[:count], shapes)]
    return weights, out[count:]


def per_device(
    tokens,
    gain_mix,
    in_weight,
    conv_weight,
    out_weight,
    gain_ff,
    gate_up_weight,
    down_weight,
    grad_out,
):
    inputs = tokens.astype(jnp.float32)
    dp, tensor = lax.axis_size("dp"), lax.axis_size("tensor")
    weights, kept = gather_forward(
        [in_weight, out_weight[None], gate_up_weight, down_weight[None]],
        tokens,
        gain_mix,
        conv_weight,
        gain_ff,
        GROUPS,
        STARTS,
        dp,
        tensor,
    )
    in_full, out_full, gate_up_full, down_full = weights
    normed_mix, projected, gated_rows, residual, normed_ff, gate_low, up_low, hidden = kept
    projected = projected.astype(jnp.float32)
    out_full, down_full = out_full[0], down_full[0]
    rows, width = tokens.shape
    seq_count = rows // LEN
    scale_mix = norm_scale(inputs)
    shaped = (seq_count, LEN, width)
    input_gate = projected[0].reshape(shaped)
    output_gate = projected[1].reshape(shaped)
    value_part = projected[2].reshape(shaped)
    mixed_in = input_gate * value_part
    conv_out = (
        conv_weight[0] * delayed(mixed_in, 2)
        + conv_weight[1] * delayed(mixed_in, 1)
        + conv_weight[2] * mixed_in
    )
    scale_ff = norm_scale(residual)
    gate_pre = gate_low.astype(jnp.float32)
    up_value = up_low.astype(jnp.float32)
    sigmoid_gate = jax.nn.sigmoid(gate_pre)
    silu_gate = gate_pre * sigmoid_gate
    block_out = (
        residual
        + lax.dot_general(
            hidden, down_full, (((1,), (1,)), ((), ())), preferred_element_type=jnp.float32
        )
    ).astype(jnp.bfloat16)
    hidden_grad = jnp.dot(grad_out, down_full, preferred_element_type=jnp.float32)
    silu_slope = sigmoid_gate * (1.0 + gate_pre * (1.0 - sigmoid_gate))
    gate_grad = (hidden_grad * up_value * silu_slope).astype(jnp.bfloat16)
    up_grad = (hidden_grad * silu_gate).astype(jnp.bfloat16)
    gate_up_grad = jnp.stack([gate_grad, up_grad])
    ffn_in_grad = jnp.einsum(
        "jgf,jdf->gd", gate_up_grad, gate_up_full, preferred_element_type=jnp.float32
    )
    residual_back, gain_ff_grad = norm_back(residual, scale_ff, gain_ff, ffn_in_grad)
    residual_grad = grad_out.astype(jnp.float32) + residual_back
    mixer_grads = residual_grad.astype(jnp.bfloat16)
    gated_grad = jnp.dot(mixer_grads, out_full, preferred_element_type=jnp.float32).reshape(shaped)
    output_gate_grad = gated_grad * conv_out
    conv_grad_in = gated_grad * output_gate
    mixed_grad = (
        conv_weight[2] * conv_grad_in
        + conv_weight[1] * advanced(conv_grad_in, 1)
        + conv_weight[0] * advanced(conv_grad_in, 2)
    )
    tap_grads = jnp.stack(
        [
            jnp.sum(conv_grad_in * delayed(mixed_in, 2), axis=(0, 1)),
            jnp.sum(conv_grad_in * delayed(mixed_in, 1), axis=(0, 1)),
            jnp.sum(conv_grad_in * mixed_in, axis=(0, 1)),
        ]
    )
    proj_grad = (
        jnp.stack([mixed_grad * value_part, output_gate_grad, mixed_grad * input_gate])
        .astype(jnp.bfloat16)
        .reshape(3, rows, width)
    )
    mixer_in_grad = jnp.einsum(
        "jgc,jdc->gd", proj_grad, in_full, preferred_element_type=jnp.float32
    )
    input_back, gain_mix_grad = norm_back(inputs, scale_mix, gain_mix, mixer_in_grad)
    input_grad = residual_grad + input_back
    small = jnp.concatenate(
        [gain_mix_grad[None], gain_ff_grad[None], tap_grads, jnp.zeros((3, width), jnp.float32)]
    )
    if in_weight.shape[1] >= 64:
        shards = (down_weight[None], gate_up_weight, in_weight, out_weight[None])
        down_sum, gate_up_sum, in_sum, out_sum, small_sums = tile_sum_all(
            [grad_out, normed_ff, normed_mix, mixer_grads],
            [hidden[None], gate_grad[None], up_grad[None], proj_grad, gated_rows[None]],
            [jax.ShapeDtypeStruct(shard.shape, jnp.float32) for shard in shards],
            PRODUCTS,
            small,
            dp,
            tensor,
        )
    else:
        down_grad = lax.dot_general(
            grad_out, hidden, (((0,), (0,)), ((), ())), preferred_element_type=jnp.float32
        )
        gate_up_weight_grad = jnp.einsum(
            "gd,jgf->jdf", normed_ff, gate_up_grad, preferred_element_type=jnp.float32
        )
        out_weight_grad = lax.dot_general(
            mixer_grads, gated_rows, (((0,), (0,)), ((), ())), preferred_element_type=jnp.float32
        )
        in_weight_grad = jnp.einsum(
            "gd,jgc->jdc", normed_mix, proj_grad, preferred_element_type=jnp.float32
        )
        down_sum, gate_up_sum, in_sum, out_sum, small_sums = sum_all(
            [
                down_grad.astype(jnp.bfloat16)[None],
                gate_up_weight_grad.astype(jnp.bfloat16),
                in_weight_grad.astype(jnp.bfloat16),
                out_weight_grad.astype(jnp.bfloat16)[None],
            ],
            small,
            SUM_GROUPS,
            dp,
            tensor,
        )
    return (
        block_out,
        input_grad,
        small_sums[0],
        in_sum,
        small_sums[2:5],
        out_sum[0],
        small_sums[1],
        gate_up_sum,
        down_sum[0],
    )


def solution(mesh):
    in_specs = (
        P(("dp", "tensor"), None),
        P(),
        P(None, "dp", "tensor"),
        P(),
        P("dp", "tensor"),
        P(),
        P(None, "dp", "tensor"),
        P("dp", "tensor"),
        P(("dp", "tensor"), None),
    )
    out_specs = (
        P(("dp", "tensor"), None),
        P(("dp", "tensor"), None),
        P(),
        P(None, "dp", "tensor"),
        P(),
        P("dp", "tensor"),
        P(),
        P(None, "dp", "tensor"),
        P("dp", "tensor"),
    )
    return jax.shard_map(
        per_device, mesh=mesh, in_specs=in_specs, out_specs=out_specs, check_vma=False
    )
```
